512 devices in a mesh: wide: 64 (over x, y, core), row: 8 (over z).
Axes of the slice: x: 4, y: 8, z: 8, core: 2. Of those that a mesh axis runs over, the one named last changes fastest.
Arguments:
- points: float32 [128, 65536], P(None, ('wide', 'row')), may hold values from -6 to 6
- targets: float32 [32, 65536], P(None, ('wide', 'row')), may hold values from -6 to 6
- lengthscales: float32 [128], replicated, may hold values from 3.5 to 7
- outputscale: float32 [1], replicated, may hold values from 0.5 to 2
- noise: float32 [1], replicated, may hold values from 0.5 to 2
Outputs:
- solution: float32 [32, 65536], P(None, ('wide', 'row'))
- residual: float32 [32, 65536], P(None, ('wide', 'row'))
The draws below stay inside these ranges and needn't reach their ends.
All inputs are finite; a program needn't handle non-finite values.
Results may differ from the reference program's by a relative error of at most 0.0003.
Values sent between devices are 32-bit elements; how exact they have to be, the bound alone decides.
No kernel may reach another device: no remote copies, remote signals or barrier semaphores. Data moves between devices by JAX's collectives and lax.ppermute only.
A program may use at most 64 MiB of HBM per device.

```python
import math
import jax
import jax.numpy as jnp
from jax import lax

D = 128
RHS = 32
ITERS = 2
POINTS = 65536
BLOCK = 1024
N_WIDE = 64


def shard_levels(key, dims, shards, least, top_value):
    def one(axis_at, parts):
        heights = jax.random.uniform(jax.random.fold_in(jax.random.fold_in(key, 6), axis_at), (parts,), jnp.float32, least / len(shards), top_value / len(shards))
        return jnp.repeat(jnp.exp(heights), dims[axis_at] // parts).reshape((-1,) + (1,) * (len(dims) - axis_at - 1))

    gain = one(*shards[0])
    for cut in shards[1:]:
        gain = gain * one(*cut)
    return gain


def scatter_about(key, dims, width, limit, split=(), kind=jnp.bfloat16):
    values = jax.random.normal(key, dims, jnp.float32) * width
    if len(split) > 0:
        values = shard_levels(key, dims, split, -0.22, 0.18) * values
    return jnp.clip(values, min=-limit, max=limit).astype(kind)


def setup_inputs(seed: int = 0) -> dict:
    key_of = jax.random.split(jax.random.key(seed), 6)
    return {
        "points": scatter_about(key_of[0], (D, POINTS), 1.0, 6.0, ((1, 512),), jnp.float32),
        "targets": scatter_about(key_of[1], (RHS, POINTS), 1.0, 6.0, ((1, 512),), jnp.float32),
        "lengthscales": jnp.clip(jnp.exp(jax.random.uniform(key_of[2], (D,), jnp.float32, math.log(3.5), math.log(7.0))), 3.5, 7.0),
        "outputscale": jnp.clip(jnp.exp(jax.random.uniform(key_of[3], (1,), jnp.float32, math.log(0.5), math.log(2.0))), 0.5, 2.0),
        "noise": jnp.clip(jnp.exp(jax.random.uniform(key_of[4], (1,), jnp.float32, math.log(0.5), math.log(2.0))), 0.5, 2.0),
    }


def kernel_rows(scaled, squares, vectors, kern_scale, start):
    left_pts = lax.dynamic_slice_in_dim(scaled, start, BLOCK, 1)
    left_sq = lax.dynamic_slice_in_dim(squares, start, BLOCK, 0)
    cross = lax.dot_general(left_pts, scaled, (((0,), (0,)), ((), ())), precision=lax.Precision.HIGHEST)
    distance = left_sq[:, None] + squares[None, :] - 2.0 * cross
    kernel = kern_scale * jnp.exp(-0.5 * distance)
    return lax.dot_general(vectors, kernel, (((1,), (1,)), ((), ())), precision=lax.Precision.HIGHEST)


def operate(scaled, squares, vectors, kern_scale, noise_var):
    starts = (jnp.arange(N_WIDE) * BLOCK).astype(jnp.int32)
    pieces = lax.map(lambda start: kernel_rows(scaled, squares, vectors, kern_scale, start), starts)
    return pieces.transpose(1, 0, 2).reshape(RHS, POINTS) + noise_var * vectors


def reference(points, targets, lengthscales, outputscale, noise):
    scaled = points / lengthscales[:, None]
    squares = jnp.sum(scaled * scaled, axis=0)
    kern_scale = outputscale[0]
    noise_var = noise[0]
    solution = jnp.zeros_like(targets)
    residual = targets
    direction = targets
    norm_now = jnp.sum(residual * residual, axis=1)
    for iteration in range(ITERS):
        image = operate(scaled, squares, direction, kern_scale, noise_var)
        step_size = norm_now / jnp.sum(direction * image, axis=1)
        solution = solution + step_size[:, None] * direction
        residual = residual - step_size[:, None] * image
        norm_next = jnp.sum(residual * residual, axis=1)
        direction = residual + (norm_next / norm_now)[:, None] * direction
        norm_now = norm_next
    return solution, residual
```

```python
import functools
import math

import jax
import jax.numpy as jnp
from jax import lax
from jax.experimental import pallas as pl
from jax.experimental.pallas import tpu as pltpu
from jax.sharding import Mesh
from jax.sharding import PartitionSpec as P

AXES = ("x", "y", "c", "z")
F32 = jnp.float32
BF16 = jnp.bfloat16
ROOT = math.sqrt(math.log2(math.e))
BLK = 128
SUB = 256


def shift(value, axis, steps):
    count = lax.axis_size(axis)
    return lax.ppermute(value, axis, [(s, (s + steps) % count) for s in range(count)])


def to_each(x, axes):
    peers = lax.axis_size(axes)
    return lax.all_to_all(jnp.broadcast_to(x[None], (peers, *x.shape)), axes, 0, 0, tiled=True)


def halves(x):
    high = x.astype(BF16)
    return high, (x - high.astype(F32)).astype(BF16)


def first_kernel(rhs, *refs):
    col_refs, row_refs = refs[0:4], refs[4:6]
    out_ref, high_ref, low_ref, left, left_sq, right, right_sq, vecs = refs[6:]
    chunk, tile = pl.program_id(0), pl.program_id(1)
    per_tile = left.shape[2] // BLK
    per_chunk = right.shape[0] // BLK

    @pl.when((chunk == 0) & (tile == 0))
    def _():
        for block in range(16):
            value = row_refs[block // 8][block % 8] * ROOT
            high, low = halves(value)
            at, lanes = block // per_tile, pl.ds(block % per_tile * BLK, BLK)
            left[at, pl.ds(0, 128), lanes] = high
            left[at, pl.ds(128, 128), lanes] = low
            left[at, pl.ds(256, 128), lanes] = high
            left[at, pl.ds(384, 128), lanes] = low
            left_sq[at, :, lanes] = -0.5 * jnp.sum(value * value, axis=0, keepdims=True)

    for which in range(4 * 8 // per_chunk):

        @pl.when((chunk == which) & (tile == 0))
        def _():
            for local in range(per_chunk):
                block = which * per_chunk + local
                ref = col_refs[block // 8]
                value = ref[block % 8, pl.ds(0, BLK), :] * ROOT
                high, low = halves(value)
                rows = pl.ds(local * BLK, BLK)
                right[rows, pl.ds(0, 128)] = high
                right[rows, pl.ds(128, 128)] = high
                right[rows, pl.ds(256, 128)] = low
                right[rows, pl.ds(384, 128)] = low
                right_sq[rows, :] = -0.5 * jnp.sum(value * value, axis=1, keepdims=True)
                high, low = halves(ref[block % 8, pl.ds(BLK, rhs), :])
                vecs[pl.ds(0, rhs), rows] = high
                vecs[pl.ds(rhs, rhs), rows] = low

    total = jnp.zeros((rhs, left.shape[2]), F32)
    for step in range(right.shape[0] // SUB):
        rows = pl.ds(step * SUB, SUB)
        power = jnp.dot(right[rows, :], left[tile], preferred_element_type=F32)
        high, low = halves(jnp.exp2(power + right_sq[rows, :] + left_sq[tile]))
        high_ref[rows, :] = high
        low_ref[rows, :] = low
        both = jnp.dot(vecs[:, rows], high, preferred_element_type=F32)
        rest = jnp.dot(vecs[pl.ds(0, rhs), rows], low, preferred_element_type=F32)
        total = total + both[:rhs] + both[rhs:] + rest
    for local in range(per_tile):
        piece = total[:, local * BLK : (local + 1) * BLK]
        at = tile * per_tile + local

        @pl.when(chunk == 0)
        def _():
            out_ref[at] = piece

        @pl.when(chunk > 0)
        def _():
            out_ref[at] = out_ref[at] + piece


def second_kernel(rhs, place_ref, gathered_ref, high_ref, low_ref, out_ref, vecs, sums):
    tile = pl.program_id(0)

    @pl.when(tile == 0)
    def _():
        place = place_ref[0]
        extra = jnp.zeros((8, BLK), F32)
        for chunk in range(4):
            source = lax.rem(place + (0, 3, 1, 2)[chunk], 4)
            for y in range(8):
                lanes = pl.ds((chunk * 8 + y) * BLK, BLK)
                high, low = halves(gathered_ref[source, y, pl.ds(0, rhs), :])
                vecs[pl.ds(0, rhs), lanes] = high
                vecs[pl.ds(rhs, rhs), lanes] = low
                extra = extra + gathered_ref[source, y, pl.ds(rhs, 8), :]
        sums[...] = extra

    both = jnp.dot(vecs[...], high_ref[...], preferred_element_type=F32)
    rest = jnp.dot(vecs[pl.ds(0, rhs), :], low_ref[...], preferred_element_type=F32)
    total = both[:rhs] + both[rhs:] + rest
    for local in range(out_ref.shape[0]):
        out_ref[local, pl.ds(0, rhs), :] = total[:, local * BLK : (local + 1) * BLK]
        out_ref[local, pl.ds(rhs, 8), :] = sums[...]


def apply_first(cols, rows, rhs):
    height, width = 4 * 8 * BLK, 16 * BLK
    chunk, tile = 2048, 512
    whole = lambda shape: pl.BlockSpec(shape, lambda j, i: (0,) * len(shape))
    return pl.pallas_call(
        functools.partial(first_kernel, rhs),
        grid=(height // chunk, width // tile),
        in_specs=[whole(c.shape) for c in cols] + [whole(r.shape) for r in rows],
        out_specs=[
            whole((16, rhs, BLK)),
            pl.BlockSpec((chunk, tile), lambda j, i: (j, i)),
            pl.BlockSpec((chunk, tile), lambda j, i: (j, i)),
        ],
        out_shape=[
            jax.ShapeDtypeStruct((16, rhs, BLK), F32),
            jax.ShapeDtypeStruct((height, width), BF16),
            jax.ShapeDtypeStruct((height, width), BF16),
        ],
        scratch_shapes=[
            pltpu.VMEM((width // tile, 512, tile), BF16),
            pltpu.VMEM((width // tile, 1, tile), F32),
            pltpu.VMEM((chunk, 512), BF16),
            pltpu.VMEM((chunk, 1), F32),
            pltpu.VMEM((2 * rhs, chunk), BF16),
        ],
        compiler_params=pltpu.CompilerParams(vmem_limit_bytes=48 << 20),
        cost_estimate=pl.CostEstimate(
            flops=2 * height * width * (512 + 256), bytes_accessed=4 * height * width, transcendentals=height * width
        ),
        name="first_product",
    )(*cols, *rows)


def apply_second(place, gathered, high, low, rhs):
    height, width = high.shape
    tile = 256
    return pl.pallas_call(
        functools.partial(second_kernel, rhs),
        grid_spec=pltpu.PrefetchScalarGridSpec(
            num_scalar_prefetch=1,
            grid=(width // tile,),
            in_specs=[
                pl.BlockSpec(gathered.shape, lambda i, p: (0, 0, 0, 0)),
                pl.BlockSpec((height, tile), lambda i, p: (0, i)),
                pl.BlockSpec((height, tile), lambda i, p: (0, i)),
            ],
            out_specs=pl.BlockSpec((tile // BLK, rhs + 8, BLK), lambda i, p: (i, 0, 0)),
            scratch_shapes=[pltpu.VMEM((2 * rhs, height), BF16), pltpu.VMEM((8, BLK), F32)],
        ),
        out_shape=jax.ShapeDtypeStruct((width // BLK, rhs + 8, BLK), F32),
        compiler_params=pltpu.CompilerParams(vmem_limit_bytes=48 << 20),
        cost_estimate=pl.CostEstimate(
            flops=2 * height * width * 128, bytes_accessed=4 * height * width, transcendentals=0
        ),
        name="second_product",
    )(place, gathered, high, low)


def owners(pieces):
    theirs = shift(pieces[8:], "c", 1)
    return jnp.sum(lax.all_to_all(pieces[:8] + theirs, "z", 0, 0, tiled=True), axis=0)


def over_all(x):
    for axes in (("y", "c"), ("x", "z")):
        x = jnp.sum(to_each(x, axes), axis=0)
    return x


def on_device(points, targets, lengthscales, outputscale, noise):
    rhs = targets.shape[0]
    scale, noise_var = outputscale[0], noise[0]
    scaled = points / lengthscales[:, None]
    near = to_each(jnp.concatenate([scaled.T, targets], axis=0), "y")
    cols = [near, shift(near, "x", 1), shift(near, "x", -1), shift(near, "x", 2)]
    scaled, near = lax.optimization_barrier((scaled, near))
    same = to_each(scaled, "z")
    other = shift(same, "c", 1)
    pieces, high, low = apply_first(cols, [same, other], rhs)
    first = scale * owners(pieces) + noise_var * targets
    dots = jnp.concatenate(
        [
            jnp.sum(targets * targets, axis=1),
            jnp.sum(targets * first, axis=1),
            jnp.sum(first * first, axis=1),
            jnp.zeros((BLK - 3 * rhs,), F32),
        ]
    )
    extra = jnp.concatenate([dots[None], jnp.zeros((7, BLK), F32)], axis=0)
    gathered = to_each(jnp.concatenate([first, extra], axis=0), ("x", "y")).reshape(4, 8, rhs + 8, BLK)
    place = lax.axis_index("x").astype(jnp.int32)[None]
    summed = owners(apply_second(place, gathered, high, low, rhs))
    second = scale * summed[:rhs] + noise_var * first
    dots = summed[rhs]
    norm, curve, image_sq = dots[:rhs], dots[rhs : 2 * rhs], dots[2 * rhs : 3 * rhs]
    step = norm / curve
    ratio = (norm - 2.0 * step * curve + step * step * image_sq) / norm
    step, ratio = step[:, None], ratio[:, None]
    residual = targets - step * first
    direction = residual + ratio * targets
    image = first - step * second + ratio * first
    new_curve = over_all(jnp.sum(direction * image, axis=1)[None])[0]
    new_step = (ratio[:, 0] * norm / new_curve)[:, None]
    return (step * targets + new_step * direction, residual - new_step * image)


def solution(mesh):
    finer = Mesh(mesh.devices.reshape(4, 8, 2, mesh.shape["row"]), AXES)
    spec = P(None, AXES)
    return jax.shard_map(
        on_device, mesh=finer, in_specs=(spec, spec, P(), P(), P()), out_specs=(spec, spec), check_vma=False
    )
```

```python
import functools
import math

import jax
import jax.numpy as jnp
from jax import lax
from jax.experimental import pallas as pl
from jax.experimental.pallas import tpu as pltpu
from jax.sharding import Mesh
from jax.sharding import PartitionSpec as P

AXES = ("x", "y", "c", "z")
F32 = jnp.float32
BF16 = jnp.bfloat16
ROOT = math.sqrt(math.log2(math.e))
BLK = 128
RHS = 32
EXTRA = 8
TILE = 512
SUB = 512
WIDE = 1024
VMEM = pl.BlockSpec(memory_space=pltpu.VMEM)
SMEM = pl.BlockSpec(memory_space=pltpu.SMEM)
PARAMS = pltpu.CompilerParams(vmem_limit_bytes=12 << 20)


def shift(value, axis, steps):
    count = lax.axis_size(axis)
    return lax.ppermute(value, axis, [(s, (s + steps) % count) for s in range(count)])


def exchange(x, axes):
    return lax.all_to_all(x, axes, 0, 0, tiled=True)


def halves(x):
    high = x.astype(BF16)
    return high, (x - high.astype(F32)).astype(BF16)


def kept(x):
    return pltpu.with_memory_space_constraint(x, pltpu.VMEM)


def cost(flops=0, moved=0, powers=0):
    return pl.CostEstimate(flops=flops, bytes_accessed=moved, transcendentals=powers)


def spread_kernel(points, lengths, targets, scale, noise, out, own, aux):
    scaled = points[...] / lengths[...]
    vectors = targets[...]
    own[...] = scaled
    for peer in range(8):
        out[peer, pl.ds(0, BLK), :] = scaled
        out[peer, pl.ds(BLK, RHS), :] = vectors
    aux[...] = jnp.where(lax.broadcasted_iota(jnp.int32, (8, BLK), 0) == 0, scale[0], noise[0])


def spread(points, lengths, targets, scale, noise):
    return pl.pallas_call(
        spread_kernel,
        in_specs=[VMEM, VMEM, VMEM, SMEM, SMEM],
        out_specs=[VMEM] * 3,
        out_shape=[
            jax.ShapeDtypeStruct((8, BLK + RHS, BLK), F32),
            jax.ShapeDtypeStruct((BLK, BLK), F32),
            jax.ShapeDtypeStruct((8, BLK), F32),
        ],
        compiler_params=PARAMS,
        name="spread",
    )(points, lengths, targets, scale, noise)


ORDER = (0, -1, 1, 4, -3, -2, 2, 3)


def prepare_rows(place, row_refs, left, left_sq):
    for block in range(16):
        value = row_refs[block // 8][block % 8] * ROOT
        high, low = halves(value)
        z = lax.rem(place[0] + (ORDER[block % 8] + 8), 8)
        at = block // 8 * 2 + lax.div(z, 4)
        lanes = pl.ds(pl.multiple_of(lax.rem(z, 4) * BLK, BLK), BLK)
        left[at, pl.ds(0, 128), lanes] = high
        left[at, pl.ds(128, 128), lanes] = low
        left[at, pl.ds(256, 128), lanes] = high
        left[at, pl.ds(384, 128), lanes] = low
        left_sq[at, :, lanes] = -0.5 * jnp.sum(value * value, axis=0, keepdims=True)


def prepare_cols(col_refs, right, right_sq, vecs):
    each = 8 // len(col_refs)
    for block in range(8):
        ref, at = col_refs[block // each], block % each
        value = ref[at, pl.ds(0, BLK), :].T * ROOT
        high, low = halves(value)
        rows = pl.ds(block * BLK, BLK)
        right[rows, pl.ds(0, 128)] = high
        right[rows, pl.ds(128, 128)] = high
        right[rows, pl.ds(256, 128)] = low
        right[rows, pl.ds(384, 128)] = low
        right_sq[rows, :] = -0.5 * jnp.sum(value * value, axis=1, keepdims=True)
        high, low = halves(ref[at, pl.ds(BLK, RHS), :])
        vecs[pl.ds(0, RHS), rows] = high
        vecs[pl.ds(RHS, RHS), rows] = low


def make_values(left, left_sq, right, right_sq, vecs, high_ref, low_ref, out, before):
    def one(tile, carry):
        total = jnp.zeros((RHS, TILE), F32)
        for step in range(WIDE // SUB):
            rows = pl.ds(step * SUB, SUB)
            power = jnp.dot(right[rows, :], left[tile], preferred_element_type=F32)
            high, low = halves(jnp.exp2(power + right_sq[rows, :] + left_sq[tile]))
            high_ref[tile, rows, :] = high
            low_ref[tile, rows, :] = low
            both = jnp.dot(vecs[:, rows], high, preferred_element_type=F32)
            rest = jnp.dot(vecs[pl.ds(0, RHS), rows], low, preferred_element_type=F32)
            total = total + both[:RHS] + both[RHS:] + rest
        for local in range(TILE // BLK):
            at = tile * (TILE // BLK) + local
            piece = total[:, local * BLK : (local + 1) * BLK]
            out[at] = piece if before is None else piece + before[at]
        return carry

    lax.fori_loop(0, 4, one, 0)


def own_kernel(place, cols, same, other, out, high, low, left, left_sq, right, right_sq, vecs):
    prepare_rows(place, (same, other), left, left_sq)
    prepare_cols((cols,), right, right_sq, vecs)
    make_values(left, left_sq, right, right_sq, vecs, high, low, out, None)


def more_kernel(count, *refs):
    cols, (left, left_sq, before, out, high, low, right, right_sq, vecs) = refs[:count], refs[count:]
    prepare_cols(cols, right, right_sq, vecs)
    make_values(left, left_sq, right, right_sq, vecs, high, low, out, before)


PIECES = pltpu.VMEM((16, RHS, BLK), F32)
VALUES = pltpu.VMEM((4, WIDE, TILE), BF16)
LEFT = [pltpu.VMEM((4, 512, TILE), BF16), pltpu.VMEM((4, 1, TILE), F32)]
RIGHT = [pltpu.VMEM((WIDE, 512), BF16), pltpu.VMEM((WIDE, 1), F32), pltpu.VMEM((2 * RHS, WIDE), BF16)]
CHUNK_COST = cost(2 * 2048 * WIDE * 768, 4 * 2048 * WIDE, 2048 * WIDE)


def own_chunk(place, cols, same, other):
    return pl.pallas_call(
        own_kernel,
        in_specs=[SMEM] + [VMEM] * 3,
        out_specs=[VMEM] * 5,
        out_shape=[PIECES, VALUES, VALUES, *LEFT],
        scratch_shapes=RIGHT,
        compiler_params=PARAMS,
        cost_estimate=CHUNK_COST,
        name="own_chunk",
    )(place, cols, same, other)


def more_chunk(cols, left, left_sq, before):
    return pl.pallas_call(
        functools.partial(more_kernel, len(cols)),
        in_specs=[VMEM] * (len(cols) + 3),
        out_specs=[VMEM] * 3,
        out_shape=[PIECES, VALUES, VALUES],
        scratch_shapes=RIGHT,
        compiler_params=PARAMS,
        cost_estimate=CHUNK_COST,
        name="more_chunk",
    )(*cols, kept(left), kept(left_sq), kept(before))


def as_rows(columns):
    lane = lax.broadcasted_iota(jnp.int32, (RHS, BLK), 1)
    wide = jnp.zeros((RHS, BLK), F32)
    for at, column in enumerate(columns):
        wide = jnp.where(lane == at, column, wide)
    return jnp.concatenate([wide, jnp.zeros((BLK - RHS, BLK), F32)], axis=0).T[:EXTRA]


def as_columns(rows, count):
    tall = jnp.concatenate([rows, jnp.zeros((BLK - rows.shape[0], BLK), F32)], axis=0).T
    return [tall[:RHS, at : at + 1] for at in range(count)]


def total(x):
    return jnp.sum(x, axis=1, keepdims=True)


def between_kernel(aux, arrived, targets, first_ref, wide_ref):
    vectors = targets[...]
    first = aux[0:1, 0:1] * jnp.sum(arrived[...], axis=0) + aux[1:2, 0:1] * vectors
    extra = as_rows([total(vectors * vectors), total(vectors * first), total(first * first)])
    first_ref[...] = first
    for peer in range(8):
        wide_ref[peer, pl.ds(0, RHS), :] = first
        wide_ref[peer, pl.ds(RHS, EXTRA), :] = extra


def between(aux, arrived, targets):
    return pl.pallas_call(
        between_kernel,
        in_specs=[VMEM] * 3,
        out_specs=[VMEM] * 2,
        out_shape=[
            jax.ShapeDtypeStruct((RHS, BLK), F32),
            jax.ShapeDtypeStruct((8, RHS + EXTRA, BLK), F32),
        ],
        compiler_params=PARAMS,
        name="between",
    )(aux, arrived, targets)


def second_kernel(tiles, count, *refs):
    vectors, highs, lows = refs[:count], refs[count : 2 * count], refs[2 * count : 3 * count]
    before, out, vecs = refs[3 * count :] if len(refs) > 3 * count + 2 else (None, *refs[3 * count :])
    sums = jnp.zeros((EXTRA, BLK), F32)
    for chunk in range(count):
        for y in range(8):
            lanes = pl.ds(y * BLK, BLK)
            high, low = halves(vectors[chunk][y, pl.ds(0, RHS), :])
            vecs[chunk, pl.ds(0, RHS), lanes] = high
            vecs[chunk, pl.ds(RHS, RHS), lanes] = low
            sums = sums + vectors[chunk][y, pl.ds(RHS, EXTRA), :]
    for at, tile in enumerate(tiles):
        product = jnp.zeros((RHS, TILE), F32)
        for chunk in range(count):
            both = jnp.dot(vecs[chunk], highs[chunk][tile], preferred_element_type=F32)
            rest = jnp.dot(vecs[chunk, pl.ds(0, RHS), :], lows[chunk][tile], preferred_element_type=F32)
            product = product + both[:RHS] + both[RHS:] + rest
        for local in range(TILE // BLK):
            to = at * (TILE // BLK) + local
            from_ = tile * (TILE // BLK) + local
            piece = product[:, local * BLK : (local + 1) * BLK]
            if before is None:
                out[to, pl.ds(0, RHS), :] = piece
                out[to, pl.ds(RHS, EXTRA), :] = sums
            else:
                out[to, pl.ds(0, RHS), :] = piece + before[from_, pl.ds(0, RHS), :]
                out[to, pl.ds(RHS, EXTRA), :] = sums + before[from_, pl.ds(RHS, EXTRA), :]


def second(tiles, vectors, highs, lows, before=None):
    count = len(vectors)
    more = [] if before is None else [kept(before)]
    return pl.pallas_call(
        functools.partial(second_kernel, tiles, count),
        in_specs=[VMEM] * (3 * count + len(more)),
        out_specs=VMEM,
        out_shape=pltpu.VMEM((len(tiles) * 4, RHS + EXTRA, BLK), F32),
        scratch_shapes=[pltpu.VMEM((count, 2 * RHS, WIDE), BF16)],
        compiler_params=PARAMS,
        cost_estimate=cost(2 * 512 * len(tiles) * WIDE * count * 128, 4 * 512 * len(tiles) * WIDE * count, 0),
        name=f"second_{len(tiles)}x{count}",
    )(*vectors, *[kept(v) for v in highs], *[kept(v) for v in lows], *more)


def steps(extra):
    norm, curve, image_sq = as_columns(extra, 3)
    step = norm / curve
    norm_next = norm - 2.0 * step * curve + step * step * image_sq
    return step, norm_next, norm_next / norm


def settle_kernel(aux, arrived, targets, first, moves_ref, form_ref):
    whole = jnp.sum(arrived[...], axis=0)
    vectors, image = targets[...], first[...]
    second_image = aux[0:1, 0:1] * whole[:RHS] + aux[1:2, 0:1] * image
    step, norm_next, ratio = steps(whole[RHS:])
    residual = vectors - step * image
    direction = residual + ratio * vectors
    moved = image - step * second_image + ratio * image
    moves_ref[0] = step * vectors
    moves_ref[1] = residual
    moves_ref[2] = direction
    moves_ref[3] = moved
    moves_ref[4] = jnp.broadcast_to(norm_next, (RHS, BLK))
    form_ref[...] = as_rows([total(direction * moved)])


def settle(aux, arrived, targets, first):
    return pl.pallas_call(
        settle_kernel,
        in_specs=[VMEM] * 4,
        out_specs=[VMEM] * 2,
        out_shape=[jax.ShapeDtypeStruct((5, RHS, BLK), F32), jax.ShapeDtypeStruct((EXTRA, BLK), F32)],
        compiler_params=PARAMS,
        name="settle",
    )(aux, arrived, targets, first)


def finish_kernel(forms, moves, solution_ref, residual_ref):
    (curve,) = as_columns(jnp.sum(forms[...], axis=0), 1)
    step = moves[4][:, 0:1] / curve
    solution_ref[...] = moves[0] + step * moves[2]
    residual_ref[...] = moves[1] - step * moves[3]


def finish(forms, moves):
    shape = jax.ShapeDtypeStruct((RHS, BLK), F32)
    return pl.pallas_call(
        finish_kernel,
        in_specs=[VMEM] * 2,
        out_specs=[VMEM] * 2,
        out_shape=[shape, shape],
        compiler_params=PARAMS,
        name="finish",
    )(forms, moves)


def to_each(x, axes):
    peers = lax.axis_size(axes)
    return exchange(jnp.broadcast_to(x[None], (peers, *x.shape)), axes)


def on_device(points, targets, lengthscales, outputscale, noise):
    near, own, aux = spread(points, lengthscales[:, None], targets, outputscale, noise)
    near = exchange(near, "y")
    behind, ahead, across = shift(near, "x", 1), shift(near, "x", -1), shift(near, "x", 2)
    below, above, far = shift(own, "z", 1), shift(own, "z", -1), shift(own, "z", 4)
    pairs = [shift(jnp.stack([below, own]), "z", 2), shift(jnp.stack([own, above]), "z", -2)]
    same = jnp.concatenate([jnp.stack([own, below, above, far]), *pairs])
    other = shift(same, "c", 1)
    place = lax.axis_index("z").astype(jnp.int32)[None]
    pieces, high, low, left, left_sq = own_chunk(place, near, same, other)
    highs, lows = [high], [low]
    for cols in (behind, ahead, across):
        pieces, high, low = more_chunk([cols], left, left_sq, pieces)
        highs.append(high)
        lows.append(low)
    arrived = exchange(pieces[:8] + shift(pieces[8:], "c", 1), "z")
    first, wide = between(aux, arrived, targets)
    near = exchange(wide, "y")
    gathered = [shift(near, "x", 1), shift(near, "x", -1), shift(near, "x", 2)]
    before = second((0, 1, 2, 3), [near], highs[:1], lows[:1])
    theirs = shift(second((2, 3), gathered, highs[1:], lows[1:], before), "c", 1)
    mine = second((0, 1), gathered, highs[1:], lows[1:], before)
    arrived = exchange(mine + theirs, "z")
    moves, form = settle(aux, arrived, targets, first)
    form = jnp.sum(to_each(form[0:1], ("y", "c")), axis=0)
    return tuple(finish(to_each(form, ("x", "z")), moves))


def solution(mesh):
    finer = Mesh(mesh.devices.reshape(4, 8, 2, mesh.shape["row"]), AXES)
    spec = P(None, AXES)
    return jax.shard_map(
        on_device, mesh=finer, in_specs=(spec, spec, P(), P(), P()), out_specs=(spec, spec), check_vma=False
    )
```

```python
import functools
import math

import jax
import jax.numpy as jnp
from jax import lax
from jax.experimental import pallas as pl
from jax.experimental.pallas import tpu as pltpu
from jax.sharding import Mesh
from jax.sharding import PartitionSpec as P


AXES = ("x", "y", "c", "z")
F32 = jnp.float32
BF16 = jnp.bfloat16
ROOT = math.sqrt(math.log2(math.e))
BLK = 128
RHS = 32
TILE = 512
SUB = 512
WIDE = 1024
VMEM = pl.BlockSpec(memory_space=pltpu.VMEM)
SMEM = pl.BlockSpec(memory_space=pltpu.SMEM)
PARAMS = pltpu.CompilerParams(vmem_limit_bytes=12 << 20)


def shift(value, axis, steps):
    count = lax.axis_size(axis)
    return lax.ppermute(value, axis, [(s, (s + steps) % count) for s in range(count)])


def exchange(x, axes):
    return lax.all_to_all(x, axes, 0, 0, tiled=True)


def halves(x):
    high = x.astype(BF16)
    return high, (x - high.astype(F32)).astype(BF16)


def kept(x):
    return pltpu.with_memory_space_constraint(x, pltpu.VMEM)


def cost(flops=0, moved=0, powers=0):
    return pl.CostEstimate(flops=flops, bytes_accessed=moved, transcendentals=powers)


def spread_kernel(points, lengths, targets, scale, noise, out, own, aux):
    scaled = points[...] / jnp.broadcast_to(lengths[...], (BLK, BLK)).T
    vectors = targets[...]
    own[...] = scaled
    for peer in range(8):
        out[peer, pl.ds(0, BLK), :] = scaled
        out[peer, pl.ds(BLK, RHS), :] = vectors
    aux[...] = jnp.where(lax.broadcasted_iota(jnp.int32, (8, BLK), 0) == 0, scale[0], noise[0])


def spread(points, lengths, targets, scale, noise):
    return pl.pallas_call(
        spread_kernel,
        in_specs=[VMEM, VMEM, VMEM, SMEM, SMEM],
        out_specs=[VMEM] * 3,
        out_shape=[
            jax.ShapeDtypeStruct((8, BLK + RHS, BLK), F32),
            jax.ShapeDtypeStruct((BLK, BLK), F32),
            jax.ShapeDtypeStruct((8, BLK), F32),
        ],
        compiler_params=PARAMS,
        name="spread",
    )(points, lengths, targets, scale, noise)


ORDER = (0, -1, 1, 4, -3, -2, 2, 3)


def prepare_rows(place, row_refs, left, left_sq):
    for block in range(16):
        value = row_refs[block // 8][block % 8] * ROOT
        high, low = halves(value)
        z = lax.rem(place[0] + (ORDER[block % 8] + 8), 8)
        at = block // 8 * 2 + lax.div(z, 4)
        lanes = pl.ds(pl.multiple_of(lax.rem(z, 4) * BLK, BLK), BLK)
        left[at, pl.ds(0, 128), lanes] = high
        left[at, pl.ds(128, 128), lanes] = low
        left[at, pl.ds(256, 128), lanes] = high
        left[at, pl.ds(384, 128), lanes] = low
        left_sq[at, :, lanes] = -0.5 * jnp.sum(value * value, axis=0, keepdims=True)


def prepare_cols(col_refs, right, right_sq, vecs):
    each = 8 // len(col_refs)
    for block in range(8):
        ref, at = col_refs[block // each], block % each
        value = ref[at, pl.ds(0, BLK), :].T * ROOT
        high, low = halves(value)
        rows = pl.ds(block * BLK, BLK)
        right[rows, pl.ds(0, 128)] = high
        right[rows, pl.ds(128, 128)] = high
        right[rows, pl.ds(256, 128)] = low
        right[rows, pl.ds(384, 128)] = low
        right_sq[rows, :] = -0.5 * jnp.sum(value * value, axis=1, keepdims=True)
        high, low = halves(ref[at, pl.ds(BLK, RHS), :])
        vecs[pl.ds(0, RHS), rows] = high
        vecs[pl.ds(RHS, RHS), rows] = low


def make_values(tiles, left, left_sq, right, right_sq, vecs, high_ref, low_ref, out, before):
    def one(to, carry):
        tile = tiles[0] + to
        total = jnp.zeros((RHS, TILE), F32)
        for step in range(WIDE // SUB):
            rows = pl.ds(step * SUB, SUB)
            power = jnp.dot(right[rows, :], left[tile], preferred_element_type=F32)
            high, low = halves(jnp.exp2(power + right_sq[rows, :] + left_sq[tile]))
            high_ref[to, rows, :] = high
            low_ref[to, rows, :] = low
            both = jnp.dot(vecs[:, rows], high, preferred_element_type=F32)
            rest = jnp.dot(vecs[pl.ds(0, RHS), rows], low, preferred_element_type=F32)
            total = total + both[:RHS] + both[RHS:] + rest
        for local in range(TILE // BLK):
            piece = total[:, local * BLK : (local + 1) * BLK]
            if before is not None:
                piece = piece + before[tile * (TILE // BLK) + local]
            out[to * (TILE // BLK) + local] = piece
        return carry

    lax.fori_loop(0, len(tiles), one, 0)


def own_kernel(place, cols, same, other, out, high, low, left, left_sq, right, right_sq, vecs):
    prepare_rows(place, (same, other), left, left_sq)
    prepare_cols((cols,), right, right_sq, vecs)
    make_values(ALL, left, left_sq, right, right_sq, vecs, high, low, out, None)


def more_kernel(tiles, cols, left, left_sq, before, out, high, low, right, right_sq, vecs):
    prepare_cols((cols,), right, right_sq, vecs)
    make_values(tiles, left, left_sq, right, right_sq, vecs, high, low, out, before)


ALL, MINE, THEIRS = (0, 1, 2, 3), (0, 1), (2, 3)


def made(tiles):
    values = pltpu.VMEM((len(tiles), WIDE, TILE), BF16)
    return [pltpu.VMEM((len(tiles) * TILE // BLK, RHS, BLK), F32), values, values]


def made_cost(tiles):
    width = len(tiles) * TILE
    return cost(2 * width * WIDE * 768, 4 * width * WIDE, width * WIDE)


LEFT = [pltpu.VMEM((4, 512, TILE), BF16), pltpu.VMEM((4, 1, TILE), F32)]
RIGHT = [pltpu.VMEM((WIDE, 512), BF16), pltpu.VMEM((WIDE, 1), F32), pltpu.VMEM((2 * RHS, WIDE), BF16)]


def own_chunk(place, cols, same, other):
    return pl.pallas_call(
        own_kernel,
        in_specs=[SMEM] + [VMEM] * 3,
        out_specs=[VMEM] * 5,
        out_shape=[*made(ALL), *LEFT],
        scratch_shapes=RIGHT,
        compiler_params=PARAMS,
        cost_estimate=made_cost(ALL),
        name="own_chunk",
    )(place, cols, same, other)


def more_chunk(tiles, cols, left, left_sq, before):
    return pl.pallas_call(
        functools.partial(more_kernel, tiles),
        in_specs=[VMEM] * 4,
        out_specs=[VMEM] * 3,
        out_shape=made(tiles),
        scratch_shapes=RIGHT,
        compiler_params=PARAMS,
        cost_estimate=made_cost(tiles),
    )(cols, kept(left), kept(left_sq), kept(before))


def total(x):
    return jnp.sum(x, axis=1, keepdims=True)


def between_kernel(aux, arrived, targets, first_ref, wide_ref):
    first = aux[0:1, 0:1] * jnp.sum(arrived[...], axis=0) + aux[1:2, 0:1] * targets[...]
    first_ref[...] = first
    for peer in range(32):
        wide_ref[peer] = first


def between(aux, arrived, targets):
    return pl.pallas_call(
        between_kernel,
        in_specs=[VMEM] * 3,
        out_specs=[VMEM] * 2,
        out_shape=[jax.ShapeDtypeStruct((RHS, BLK), F32), jax.ShapeDtypeStruct((32, RHS, BLK), F32)],
        compiler_params=PARAMS,
        name="between",
    )(aux, arrived, targets)


def second_kernel(tiles, gathered, *refs):
    highs, lows, out, vecs = refs[0:4], refs[4:8], refs[8], refs[9]
    place = lax.axis_index("x")
    for chunk in range(4):
        source = lax.rem(place + (0, 3, 1, 2)[chunk], 4) * 8
        for y in range(8):
            lanes = pl.ds(y * BLK, BLK)
            high, low = halves(gathered[source + y])
            vecs[chunk, pl.ds(0, RHS), lanes] = high
            vecs[chunk, pl.ds(RHS, RHS), lanes] = low
    for to, tile in enumerate(tiles):
        product = jnp.zeros((RHS, TILE), F32)
        for chunk in range(4):
            at = to if chunk == 3 else tile
            both = jnp.dot(vecs[chunk], highs[chunk][at], preferred_element_type=F32)
            rest = jnp.dot(vecs[chunk, pl.ds(0, RHS), :], lows[chunk][at], preferred_element_type=F32)
            product = product + both[:RHS] + both[RHS:] + rest
        for local in range(TILE // BLK):
            out[to * (TILE // BLK) + local] = product[:, local * BLK : (local + 1) * BLK]


def second(tiles, gathered, highs, lows):
    width = len(tiles) * TILE
    return pl.pallas_call(
        functools.partial(second_kernel, tiles),
        in_specs=[VMEM] * 9,
        out_specs=VMEM,
        out_shape=pltpu.VMEM((width // BLK, RHS, BLK), F32),
        scratch_shapes=[pltpu.VMEM((4, 2 * RHS, WIDE), BF16)],
        compiler_params=PARAMS,
        cost_estimate=cost(2 * width * 4 * WIDE * 128, 4 * width * 4 * WIDE, 0),
    )(gathered, *[kept(v) for v in highs], *[kept(v) for v in lows])


def total(x):
    return jnp.sum(x, axis=1, keepdims=True)


def settle_kernel(aux, arrived, targets, first_ref, second_ref, dots_ref):
    vectors, first = targets[...], first_ref[...]
    second_image = aux[0:1, 0:1] * jnp.sum(arrived[...], axis=0) + aux[1:2, 0:1] * first
    second_ref[...] = second_image
    dots = (vectors * vectors, vectors * first, first * first, first * second_image)
    lane = lax.broadcasted_iota(jnp.int32, (RHS, BLK), 1)
    wide = jnp.zeros((RHS, BLK), F32)
    for at, dot in enumerate(dots):
        wide = jnp.where(lane == at, total(dot), wide)
    tall = jnp.concatenate([wide, jnp.zeros((BLK - RHS, BLK), F32)], axis=0).T
    row = tall[0:1]
    for at in range(1, 4):
        row = row + pltpu.roll(tall[at : at + 1], at * RHS, 1)
    dots_ref[...] = jnp.broadcast_to(row, (8, BLK))


def settle(aux, arrived, targets, first):
    return pl.pallas_call(
        settle_kernel,
        in_specs=[VMEM] * 4,
        out_specs=[VMEM] * 2,
        out_shape=[jax.ShapeDtypeStruct((RHS, BLK), F32), jax.ShapeDtypeStruct((8, BLK), F32)],
        compiler_params=PARAMS,
        name="settle",
    )(aux, arrived, targets, first)


def finish_kernel(sums, targets, first_ref, second_ref, solution_ref, residual_ref):
    row = jnp.broadcast_to(jnp.sum(sums[...], axis=0), (8, BLK))
    sub = lax.broadcasted_iota(jnp.int32, (8, BLK), 0)
    rows = jnp.zeros((8, BLK), F32)
    for at in range(4):
        rows = jnp.where(sub == at, pltpu.roll(row, (BLK - at * RHS) % BLK, 1), rows)
    tall = jnp.concatenate([rows, jnp.zeros((BLK - 8, BLK), F32)], axis=0).T
    norm, curve, square, cubic = [tall[:RHS, at : at + 1] for at in range(4)]
    vectors, first = targets[...], first_ref[...]
    step = norm / curve
    norm_next = norm - 2.0 * step * curve + step * step * square
    more = 1.0 + norm_next / norm
    new_curve = more * more * curve - 2.0 * step * more * square + step * step * cubic
    new_step = norm_next / new_curve
    solution_ref[...] = step * vectors + new_step * (more * vectors - step * first)
    residual_ref[...] = vectors - step * first - new_step * (more * first - step * second_ref[...])


def finish(sums, targets, first, second_image):
    shape = jax.ShapeDtypeStruct((RHS, BLK), F32)
    return pl.pallas_call(
        finish_kernel,
        in_specs=[VMEM] * 4,
        out_specs=[VMEM] * 2,
        out_shape=[shape, shape],
        compiler_params=PARAMS,
        name="finish",
    )(sums, targets, first, second_image)


def to_each(x, axes):
    peers = lax.axis_size(axes)
    return exchange(jnp.broadcast_to(x[None], (peers, *x.shape)), axes)


def on_device(points, targets, lengthscales, outputscale, noise):
    near, own, aux = spread(points, lengthscales[None], targets, outputscale, noise)
    near = exchange(near, "y")
    behind, ahead, across = shift(near, "x", 1), shift(near, "x", -1), shift(near, "x", 2)
    below, above, far = shift(own, "z", 1), shift(own, "z", -1), shift(own, "z", 4)
    pairs = [shift(jnp.stack([below, own]), "z", 2), shift(jnp.stack([own, above]), "z", -2)]
    same = jnp.concatenate([jnp.stack([own, below, above, far]), *pairs])
    other = shift(same, "c", 1)
    place = lax.axis_index("z").astype(jnp.int32)[None]
    pieces, high, low, left, left_sq = own_chunk(place, near, same, other)
    highs, lows = [high], [low]
    for cols in (behind, ahead):
        pieces, high, low = more_chunk(ALL, cols, left, left_sq, pieces)
        highs.append(high)
        lows.append(low)
    theirs, high_theirs, low_theirs = more_chunk(THEIRS, across, left, left_sq, pieces)
    theirs = shift(theirs, "c", 1)
    mine, high_mine, low_mine = more_chunk(MINE, across, left, left_sq, pieces)
    arrived = exchange(mine + theirs, "z")
    first, wide = between(aux, arrived, targets)
    gathered = exchange(wide, ("x", "y"))
    theirs = shift(second(THEIRS, gathered, highs + [high_theirs], lows + [low_theirs]), "c", 1)
    mine = second(MINE, gathered, highs + [high_mine], lows + [low_mine])
    arrived = exchange(mine + theirs, "z")
    second_image, dots = settle(aux, arrived, targets, first)
    sums = jnp.sum(to_each(dots[0:1], ("y", "c")), axis=0)
    return tuple(finish(to_each(sums, ("x", "z")), targets, first, second_image))


def solution(mesh):
    finer = Mesh(mesh.devices.reshape(4, 8, 2, mesh.shape["row"]), AXES)
    spec = P(None, AXES)

    return jax.shard_map(
        on_device, mesh=finer, in_specs=(spec, spec, P(), P(), P()), out_specs=(spec, spec), check_vma=False
    )
```

```python
import functools
import math

import jax
import jax.numpy as jnp
from jax import lax
from jax.experimental import pallas as pl
from jax.experimental.pallas import tpu as pltpu
from jax.sharding import Mesh
from jax.sharding import PartitionSpec as P


AXES = ("x", "y", "c", "z")
F32 = jnp.float32
BF16 = jnp.bfloat16
ROOT = math.sqrt(math.log2(math.e))
BLK = 128
RHS = 32
TILE = 512
SUB = 512
WIDE = 1024
VMEM = pl.BlockSpec(memory_space=pltpu.VMEM)
SMEM = pl.BlockSpec(memory_space=pltpu.SMEM)
PARAMS = pltpu.CompilerParams(vmem_limit_bytes=12 << 20)


def shift(value, axis, steps):
    count = lax.axis_size(axis)
    return lax.ppermute(value, axis, [(s, (s + steps) % count) for s in range(count)])


def exchange(x, axes):
    return lax.all_to_all(x, axes, 0, 0, tiled=True)


def halves(x):
    high = x.astype(BF16)
    return high, (x - high.astype(F32)).astype(BF16)


def kept(x):
    return pltpu.with_memory_space_constraint(x, pltpu.VMEM)


def cost(flops=0, moved=0, powers=0):
    return pl.CostEstimate(flops=flops, bytes_accessed=moved, transcendentals=powers)


def spread_kernel(points_in, lengths_in, targets_in, scale, noise, out, own, aux, points, lengths, targets, sems):
    copies = [
        pltpu.make_async_copy(source, to, sems.at[at])
        for at, (source, to) in enumerate(((points_in, points), (lengths_in, lengths), (targets_in, targets)))
    ]
    for copy in copies:
        copy.start()
    for copy in copies:
        copy.wait()
    scaled = points[...] / jnp.broadcast_to(lengths[...], (BLK, BLK)).T
    vectors = targets[...]
    own[...] = scaled
    for peer in range(8):
        out[peer, pl.ds(0, BLK), :] = scaled
        out[peer, pl.ds(BLK, RHS), :] = vectors
    aux[...] = jnp.where(lax.broadcasted_iota(jnp.int32, (8, BLK), 0) == 0, scale[0], noise[0])


def spread(points, lengths, targets, scale, noise):
    return pl.pallas_call(
        spread_kernel,
        in_specs=[pl.BlockSpec(memory_space=pltpu.HBM)] * 3 + [SMEM, SMEM],
        out_specs=[VMEM] * 3,
        scratch_shapes=[
            pltpu.VMEM((BLK, BLK), F32),
            pltpu.VMEM((1, BLK), F32),
            pltpu.VMEM((RHS, BLK), F32),
            pltpu.SemaphoreType.DMA((3,)),
        ],
        out_shape=[
            jax.ShapeDtypeStruct((8, BLK + RHS, BLK), F32),
            jax.ShapeDtypeStruct((BLK, BLK), F32),
            jax.ShapeDtypeStruct((8, BLK), F32),
        ],
        compiler_params=PARAMS,
        name="spread",
    )(*[pltpu.with_memory_space_constraint(v, pltpu.HBM) for v in (points, lengths, targets)], scale, noise)


ORDER = (0, -1, 1, 4, -3, -2, 2, 3)


def prepare_rows(place, row_refs, left, left_sq):
    for block in range(16):
        value = row_refs[block // 8][block % 8] * ROOT
        high, low = halves(value)
        z = lax.rem(place[0] + (ORDER[block % 8] + 8), 8)
        at = block // 8 * 2 + lax.div(z, 4)
        lanes = pl.ds(pl.multiple_of(lax.rem(z, 4) * BLK, BLK), BLK)
        left[at, pl.ds(0, 128), lanes] = high
        left[at, pl.ds(128, 128), lanes] = low
        left[at, pl.ds(256, 128), lanes] = high
        left[at, pl.ds(384, 128), lanes] = low
        left_sq[at, :, lanes] = -0.5 * jnp.sum(value * value, axis=0, keepdims=True)


def prepare_cols(col_refs, right, right_sq, vecs):
    each = 8 // len(col_refs)
    for block in range(8):
        ref, at = col_refs[block // each], block % each
        value = ref[at, pl.ds(0, BLK), :].T * ROOT
        high, low = halves(value)
        rows = pl.ds(block * BLK, BLK)
        right[rows, pl.ds(0, 128)] = high
        right[rows, pl.ds(128, 128)] = high
        right[rows, pl.ds(256, 128)] = low
        right[rows, pl.ds(384, 128)] = low
        right_sq[rows, :] = -0.5 * jnp.sum(value * value, axis=1, keepdims=True)
        high, low = halves(ref[at, pl.ds(BLK, RHS), :])
        vecs[pl.ds(0, RHS), rows] = high
        vecs[pl.ds(RHS, RHS), rows] = low


def make_values(tiles, left, left_sq, right, right_sq, vecs, high_ref, low_ref, out, before):
    def one(to, carry):
        tile = tiles[0] + to
        total = jnp.zeros((RHS, TILE), F32)
        for step in range(WIDE // SUB):
            rows = pl.ds(step * SUB, SUB)
            power = jnp.dot(right[rows, :], left[tile], preferred_element_type=F32)
            high, low = halves(jnp.exp2(power + right_sq[rows, :] + left_sq[tile]))
            high_ref[to, rows, :] = high
            low_ref[to, rows, :] = low
            both = jnp.dot(vecs[:, rows], high, preferred_element_type=F32)
            rest = jnp.dot(vecs[pl.ds(0, RHS), rows], low, preferred_element_type=F32)
            total = total + both[:RHS] + both[RHS:] + rest
        for local in range(TILE // BLK):
            piece = total[:, local * BLK : (local + 1) * BLK]
            if before is not None:
                piece = piece + before[tile * (TILE // BLK) + local]
            out[to * (TILE // BLK) + local] = piece
        return carry

    lax.fori_loop(0, len(tiles), one, 0)


def own_kernel(place, cols, same, other, out, high, low, left, left_sq, right, right_sq, vecs):
    prepare_rows(place, (same, other), left, left_sq)
    prepare_cols((cols,), right, right_sq, vecs)
    make_values(ALL, left, left_sq, right, right_sq, vecs, high, low, out, None)


def more_kernel(tiles, cols, left, left_sq, before, out, high, low, right, right_sq, vecs):
    prepare_cols((cols,), right, right_sq, vecs)
    make_values(tiles, left, left_sq, right, right_sq, vecs, high, low, out, before)


ALL, MINE, THEIRS = (0, 1, 2, 3), (0, 1), (2, 3)


def made(tiles):
    values = pltpu.VMEM((len(tiles), WIDE, TILE), BF16)
    return [pltpu.VMEM((len(tiles) * TILE // BLK, RHS, BLK), F32), values, values]


def made_cost(tiles):
    width = len(tiles) * TILE
    return cost(2 * width * WIDE * 768, 4 * width * WIDE, width * WIDE)


LEFT = [pltpu.VMEM((4, 512, TILE), BF16), pltpu.VMEM((4, 1, TILE), F32)]
RIGHT = [pltpu.VMEM((WIDE, 512), BF16), pltpu.VMEM((WIDE, 1), F32), pltpu.VMEM((2 * RHS, WIDE), BF16)]


def own_chunk(place, cols, same, other):
    return pl.pallas_call(
        own_kernel,
        in_specs=[SMEM] + [VMEM] * 3,
        out_specs=[VMEM] * 5,
        out_shape=[*made(ALL), *LEFT],
        scratch_shapes=RIGHT,
        compiler_params=PARAMS,
        cost_estimate=made_cost(ALL),
        name="own_chunk",
    )(place, cols, same, other)


def more_chunk(tiles, cols, left, left_sq, before):
    return pl.pallas_call(
        functools.partial(more_kernel, tiles),
        in_specs=[VMEM] * 4,
        out_specs=[VMEM] * 3,
        out_shape=made(tiles),
        scratch_shapes=RIGHT,
        compiler_params=PARAMS,
        cost_estimate=made_cost(tiles),
    )(cols, kept(left), kept(left_sq), kept(before))


def total(x):
    return jnp.sum(x, axis=1, keepdims=True)


def between_kernel(aux, arrived, targets, first_ref, wide_ref):
    first = aux[0:1, 0:1] * jnp.sum(arrived[...], axis=0) + aux[1:2, 0:1] * targets[...]
    first_ref[...] = first
    for peer in range(32):
        wide_ref[peer] = first


def between(aux, arrived, targets):
    return pl.pallas_call(
        between_kernel,
        in_specs=[VMEM] * 3,
        out_specs=[VMEM] * 2,
        out_shape=[jax.ShapeDtypeStruct((RHS, BLK), F32), jax.ShapeDtypeStruct((32, RHS, BLK), F32)],
        compiler_params=PARAMS,
        name="between",
    )(aux, arrived, targets)


def second_kernel(tiles, gathered, *refs):
    highs, lows, out, vecs = refs[0:4], refs[4:8], refs[8], refs[9]
    place = lax.axis_index("x")
    for chunk in range(4):
        source = lax.rem(place + (0, 3, 1, 2)[chunk], 4) * 8
        for y in range(8):
            lanes = pl.ds(y * BLK, BLK)
            high, low = halves(gathered[source + y])
            vecs[chunk, pl.ds(0, RHS), lanes] = high
            vecs[chunk, pl.ds(RHS, RHS), lanes] = low
    for to, tile in enumerate(tiles):
        product = jnp.zeros((RHS, TILE), F32)
        for chunk in range(4):
            at = to if chunk == 3 else tile
            both = jnp.dot(vecs[chunk], highs[chunk][at], preferred_element_type=F32)
            rest = jnp.dot(vecs[chunk, pl.ds(0, RHS), :], lows[chunk][at], preferred_element_type=F32)
            product = product + both[:RHS] + both[RHS:] + rest
        for local in range(TILE // BLK):
            out[to * (TILE // BLK) + local] = product[:, local * BLK : (local + 1) * BLK]


def second(tiles, gathered, highs, lows):
    width = len(tiles) * TILE
    return pl.pallas_call(
        functools.partial(second_kernel, tiles),
        in_specs=[VMEM] * 9,
        out_specs=VMEM,
        out_shape=pltpu.VMEM((width // BLK, RHS, BLK), F32),
        scratch_shapes=[pltpu.VMEM((4, 2 * RHS, WIDE), BF16)],
        compiler_params=PARAMS,
        cost_estimate=cost(2 * width * 4 * WIDE * 128, 4 * width * 4 * WIDE, 0),
    )(gathered, *[kept(v) for v in highs], *[kept(v) for v in lows])


def total(x):
    return jnp.sum(x, axis=1, keepdims=True)


def settle_kernel(aux, arrived, targets, first_ref, second_ref, dots_ref):
    vectors, first = targets[...], first_ref[...]
    second_image = aux[0:1, 0:1] * jnp.sum(arrived[...], axis=0) + aux[1:2, 0:1] * first
    second_ref[...] = second_image
    dots = (vectors * vectors, vectors * first, first * first, first * second_image)
    lane = lax.broadcasted_iota(jnp.int32, (RHS, BLK), 1)
    wide = jnp.zeros((RHS, BLK), F32)
    for at, dot in enumerate(dots):
        wide = jnp.where(lane == at, total(dot), wide)
    tall = jnp.concatenate([wide, jnp.zeros((BLK - RHS, BLK), F32)], axis=0).T
    row = tall[0:1]
    for at in range(1, 4):
        row = row + pltpu.roll(tall[at : at + 1], at * RHS, 1)
    dots_ref[...] = jnp.broadcast_to(row, (8, BLK))


def settle(aux, arrived, targets, first):
    return pl.pallas_call(
        settle_kernel,
        in_specs=[VMEM] * 4,
        out_specs=[VMEM] * 2,
        out_shape=[jax.ShapeDtypeStruct((RHS, BLK), F32), jax.ShapeDtypeStruct((8, BLK), F32)],
        compiler_params=PARAMS,
        name="settle",
    )(aux, arrived, targets, first)


def finish_kernel(sums, targets, first_ref, second_ref, solution_ref, residual_ref):
    row = jnp.broadcast_to(jnp.sum(sums[...], axis=0), (8, BLK))
    sub = lax.broadcasted_iota(jnp.int32, (8, BLK), 0)
    rows = jnp.zeros((8, BLK), F32)
    for at in range(4):
        rows = jnp.where(sub == at, pltpu.roll(row, (BLK - at * RHS) % BLK, 1), rows)
    tall = jnp.concatenate([rows, jnp.zeros((BLK - 8, BLK), F32)], axis=0).T
    norm, curve, square, cubic = [tall[:RHS, at : at + 1] for at in range(4)]
    vectors, first = targets[...], first_ref[...]
    step = norm / curve
    norm_next = norm - 2.0 * step * curve + step * step * square
    more = 1.0 + norm_next / norm
    new_curve = more * more * curve - 2.0 * step * more * square + step * step * cubic
    new_step = norm_next / new_curve
    solution_ref[...] = step * vectors + new_step * (more * vectors - step * first)
    residual_ref[...] = vectors - step * first - new_step * (more * first - step * second_ref[...])


def finish(sums, targets, first, second_image):
    shape = jax.ShapeDtypeStruct((RHS, BLK), F32)
    return pl.pallas_call(
        finish_kernel,
        in_specs=[VMEM] * 4,
        out_specs=[VMEM] * 2,
        out_shape=[shape, shape],
        compiler_params=PARAMS,
        name="finish",
    )(sums, targets, first, second_image)


def to_each(x, axes):
    peers = lax.axis_size(axes)
    return exchange(jnp.broadcast_to(x[None], (peers, *x.shape)), axes)


def on_device(points, targets, lengthscales, outputscale, noise):
    near, own, aux = spread(points, lengthscales[None], targets, outputscale, noise)
    near = exchange(near, "y")
    behind, ahead = shift(near, "x", 1), shift(near, "x", -1)
    across = shift(near, "x", 2)
    below, above, far = shift(own, "z", 1), shift(own, "z", -1), shift(own, "z", 4)
    pairs = [shift(jnp.stack([below, own]), "z", 2), shift(jnp.stack([own, above]), "z", -2)]
    same = jnp.concatenate([jnp.stack([own, below, above, far]), *pairs])
    other = shift(same, "c", 1)
    place = lax.axis_index("z").astype(jnp.int32)[None]
    pieces, high, low, left, left_sq = own_chunk(place, near, same, other)
    highs, lows = [high], [low]
    for cols in (behind, ahead):
        pieces, high, low = more_chunk(ALL, cols, left, left_sq, pieces)
        highs.append(high)
        lows.append(low)
    theirs, high_theirs, low_theirs = more_chunk(THEIRS, across, left, left_sq, pieces)
    theirs = shift(theirs, "c", 1)
    mine, high_mine, low_mine = more_chunk(MINE, across, left, left_sq, pieces)
    arrived = exchange(mine + theirs, "z")
    first, wide = between(aux, arrived, targets)
    gathered = exchange(wide, ("x", "y"))
    theirs = shift(second(THEIRS, gathered, highs + [high_theirs], lows + [low_theirs]), "c", 1)
    mine = second(MINE, gathered, highs + [high_mine], lows + [low_mine])
    arrived = exchange(mine + theirs, "z")
    second_image, dots = settle(aux, arrived, targets, first)
    sums = jnp.sum(to_each(dots[0:1], ("y", "c")), axis=0)
    return tuple(finish(to_each(sums, ("x", "z")), targets, first, second_image))


def solution(mesh):
    finer = Mesh(mesh.devices.reshape(4, 8, 2, mesh.shape["row"]), AXES)
    spec = P(None, AXES)

    return jax.shard_map(
        on_device, mesh=finer, in_specs=(spec, spec, P(), P(), P()), out_specs=(spec, spec), check_vma=False
    )
```

```python
import functools
import math

import jax
import jax.numpy as jnp
from jax import lax
from jax.experimental import pallas as pl
from jax.experimental.pallas import tpu as pltpu
from jax.sharding import Mesh
from jax.sharding import PartitionSpec as P


AXES = ("x", "y", "c", "z")
F32 = jnp.float32
BF16 = jnp.bfloat16
ROOT = math.sqrt(math.log2(math.e))
BLK = 128
RHS = 32
TILE = 512
SUB = 512
WIDE = 1024
VMEM = pl.BlockSpec(memory_space=pltpu.VMEM)
SMEM = pl.BlockSpec(memory_space=pltpu.SMEM)
PARAMS = pltpu.CompilerParams(vmem_limit_bytes=12 << 20)


def shift(value, axis, steps):
    count = lax.axis_size(axis)
    return lax.ppermute(value, axis, [(s, (s + steps) % count) for s in range(count)])


def exchange(x, axes):
    return lax.all_to_all(x, axes, 0, 0, tiled=True)


def halves(x):
    high = x.astype(BF16)
    return high, (x - high.astype(F32)).astype(BF16)


def kept(x):
    return pltpu.with_memory_space_constraint(x, pltpu.VMEM)


def cost(flops=0, moved=0, powers=0):
    return pl.CostEstimate(flops=flops, bytes_accessed=moved, transcendentals=powers)


def spread_kernel(points_in, lengths_in, targets_in, scale, noise, out, own, aux, points, lengths, targets, sems):
    copies = [
        pltpu.make_async_copy(source, to, sems.at[at])
        for at, (source, to) in enumerate(((points_in, points), (lengths_in, lengths), (targets_in, targets)))
    ]
    for copy in copies:
        copy.start()
    for copy in copies:
        copy.wait()
    scaled = points[...] / jnp.broadcast_to(lengths[...], (BLK, BLK)).T
    vectors = targets[...]
    own[...] = scaled
    for peer in range(8):
        out[peer, pl.ds(0, BLK), :] = scaled
        out[peer, pl.ds(BLK, RHS), :] = vectors
    aux[...] = jnp.where(lax.broadcasted_iota(jnp.int32, (8, BLK), 0) == 0, scale[0], noise[0])


def spread(points, lengths, targets, scale, noise):
    return pl.pallas_call(
        spread_kernel,
        in_specs=[pl.BlockSpec(memory_space=pltpu.HBM)] * 3 + [SMEM, SMEM],
        out_specs=[VMEM] * 3,
        scratch_shapes=[
            pltpu.VMEM((BLK, BLK), F32),
            pltpu.VMEM((1, BLK), F32),
            pltpu.VMEM((RHS, BLK), F32),
            pltpu.SemaphoreType.DMA((3,)),
        ],
        out_shape=[
            jax.ShapeDtypeStruct((8, BLK + RHS, BLK), F32),
            jax.ShapeDtypeStruct((BLK, BLK), F32),
            jax.ShapeDtypeStruct((8, BLK), F32),
        ],
        compiler_params=PARAMS,
        name="spread",
    )(*[pltpu.with_memory_space_constraint(v, pltpu.HBM) for v in (points, lengths, targets)], scale, noise)


ORDER = (0, -1, 1, 4, -3, -2, 2, 3)


def prepare_rows(row_refs, left, left_sq):
    place = lax.axis_index("z")
    for block in range(16):
        value = row_refs[block // 8][block % 8] * ROOT
        high, low = halves(value)
        z = lax.rem(place + (ORDER[block % 8] + 8), 8)
        at = block // 8 * 2 + lax.div(z, 4)
        lanes = pl.ds(pl.multiple_of(lax.rem(z, 4) * BLK, BLK), BLK)
        left[at, pl.ds(0, 128), lanes] = high
        left[at, pl.ds(128, 128), lanes] = low
        left[at, pl.ds(256, 128), lanes] = high
        left[at, pl.ds(384, 128), lanes] = low
        left_sq[at, :, lanes] = -0.5 * jnp.sum(value * value, axis=0, keepdims=True)


def prepare_cols(col_refs, right, right_sq, vecs):
    each = 8 // len(col_refs)
    for block in range(8):
        ref, at = col_refs[block // each], block % each
        value = ref[at, pl.ds(0, BLK), :].T * ROOT
        high, low = halves(value)
        rows = pl.ds(block * BLK, BLK)
        right[rows, pl.ds(0, 128)] = high
        right[rows, pl.ds(128, 128)] = high
        right[rows, pl.ds(256, 128)] = low
        right[rows, pl.ds(384, 128)] = low
        right_sq[rows, :] = -0.5 * jnp.sum(value * value, axis=1, keepdims=True)
        high, low = halves(ref[at, pl.ds(BLK, RHS), :])
        vecs[pl.ds(0, RHS), rows] = high
        vecs[pl.ds(RHS, RHS), rows] = low


def make_values(tiles, left, left_sq, right, right_sq, vecs, high_ref, low_ref, out, before):
    def one(to, carry):
        tile = tiles[0] + to
        total = jnp.zeros((RHS, TILE), F32)
        for step in range(WIDE // SUB):
            rows = pl.ds(step * SUB, SUB)
            power = jnp.dot(right[rows, :], left[tile], preferred_element_type=F32)
            high, low = halves(jnp.exp2(power + right_sq[rows, :] + left_sq[tile]))
            high_ref[to, rows, :] = high
            low_ref[to, rows, :] = low
            both = jnp.dot(vecs[:, rows], high, preferred_element_type=F32)
            rest = jnp.dot(vecs[pl.ds(0, RHS), rows], low, preferred_element_type=F32)
            total = total + both[:RHS] + both[RHS:] + rest
        for local in range(TILE // BLK):
            piece = total[:, local * BLK : (local + 1) * BLK]
            if before is not None:
                piece = piece + before[tile * (TILE // BLK) + local]
            out[to * (TILE // BLK) + local] = piece
        return carry

    lax.fori_loop(0, len(tiles), one, 0)


def cols_kernel(cols, right, right_sq, vecs):
    prepare_cols((cols,), right, right_sq, vecs)


def own_kernel(same, other, right, right_sq, vecs, out, high, low, left, left_sq):
    prepare_rows((same, other), left, left_sq)
    make_values(ALL, left, left_sq, right, right_sq, vecs, high, low, out, None)


def more_kernel(tiles, cols, left, left_sq, before, out, high, low, right, right_sq, vecs):
    prepare_cols((cols,), right, right_sq, vecs)
    make_values(tiles, left, left_sq, right, right_sq, vecs, high, low, out, before)


ALL, MINE, THEIRS = (0, 1, 2, 3), (0, 1), (2, 3)


def made(tiles):
    values = pltpu.VMEM((len(tiles), WIDE, TILE), BF16)
    return [pltpu.VMEM((len(tiles) * TILE // BLK, RHS, BLK), F32), values, values]


def made_cost(tiles):
    width = len(tiles) * TILE
    return cost(2 * width * WIDE * 768, 4 * width * WIDE, width * WIDE)


LEFT = [pltpu.VMEM((4, 512, TILE), BF16), pltpu.VMEM((4, 1, TILE), F32)]
RIGHT = [pltpu.VMEM((WIDE, 512), BF16), pltpu.VMEM((WIDE, 1), F32), pltpu.VMEM((2 * RHS, WIDE), BF16)]


def own_cols(cols):
    return pl.pallas_call(
        cols_kernel,
        in_specs=[VMEM],
        out_specs=[VMEM] * 3,
        out_shape=RIGHT,
        compiler_params=PARAMS,
        cost_estimate=cost(0, 2 << 20, 0),
        name="own_cols",
    )(cols)


def own_chunk(same, other, cols):
    return pl.pallas_call(
        own_kernel,
        in_specs=[VMEM] * 5,
        out_specs=[VMEM] * 5,
        out_shape=[*made(ALL), *LEFT],
        compiler_params=PARAMS,
        cost_estimate=made_cost(ALL),
        name="own_chunk",
    )(same, other, *[kept(v) for v in cols])


def more_chunk(tiles, cols, left, left_sq, before):
    return pl.pallas_call(
        functools.partial(more_kernel, tiles),
        in_specs=[VMEM] * 4,
        out_specs=[VMEM] * 3,
        out_shape=made(tiles),
        scratch_shapes=RIGHT,
        compiler_params=PARAMS,
        cost_estimate=made_cost(tiles),
    )(cols, kept(left), kept(left_sq), kept(before))


def total(x):
    return jnp.sum(x, axis=1, keepdims=True)


def between_kernel(aux, arrived, targets, first_ref, wide_ref):
    first = aux[0:1, 0:1] * jnp.sum(arrived[...], axis=0) + aux[1:2, 0:1] * targets[...]
    first_ref[...] = first
    for peer in range(32):
        wide_ref[peer] = first


def between(aux, arrived, targets):
    return pl.pallas_call(
        between_kernel,
        in_specs=[VMEM] * 3,
        out_specs=[VMEM] * 2,
        out_shape=[jax.ShapeDtypeStruct((RHS, BLK), F32), jax.ShapeDtypeStruct((32, RHS, BLK), F32)],
        compiler_params=PARAMS,
        name="between",
    )(aux, arrived, targets)


def second_kernel(tiles, gathered, *refs):
    highs, lows, out, vecs = refs[0:4], refs[4:8], refs[8], refs[9]
    place = lax.axis_index("x")
    for chunk in range(4):
        source = lax.rem(place + (0, 3, 1, 2)[chunk], 4) * 8
        for y in range(8):
            lanes = pl.ds(y * BLK, BLK)
            high, low = halves(gathered[source + y])
            vecs[chunk, pl.ds(0, RHS), lanes] = high
            vecs[chunk, pl.ds(RHS, RHS), lanes] = low
    for to, tile in enumerate(tiles):
        product = jnp.zeros((RHS, TILE), F32)
        for chunk in range(4):
            at = to if chunk == 3 else tile
            both = jnp.dot(vecs[chunk], highs[chunk][at], preferred_element_type=F32)
            rest = jnp.dot(vecs[chunk, pl.ds(0, RHS), :], lows[chunk][at], preferred_element_type=F32)
            product = product + both[:RHS] + both[RHS:] + rest
        for local in range(TILE // BLK):
            out[to * (TILE // BLK) + local] = product[:, local * BLK : (local + 1) * BLK]


def second(tiles, gathered, highs, lows):
    width = len(tiles) * TILE
    return pl.pallas_call(
        functools.partial(second_kernel, tiles),
        in_specs=[VMEM] * 9,
        out_specs=VMEM,
        out_shape=pltpu.VMEM((width // BLK, RHS, BLK), F32),
        scratch_shapes=[pltpu.VMEM((4, 2 * RHS, WIDE), BF16)],
        compiler_params=PARAMS,
        cost_estimate=cost(2 * width * 4 * WIDE * 128, 4 * width * 4 * WIDE, 0),
    )(gathered, *[kept(v) for v in highs], *[kept(v) for v in lows])


def total(x):
    return jnp.sum(x, axis=1, keepdims=True)


def settle_kernel(aux, arrived, targets, first_ref, second_ref, dots_ref):
    vectors, first = targets[...], first_ref[...]
    second_image = aux[0:1, 0:1] * jnp.sum(arrived[...], axis=0) + aux[1:2, 0:1] * first
    second_ref[...] = second_image
    dots = (vectors * vectors, vectors * first, first * first, first * second_image)
    lane = lax.broadcasted_iota(jnp.int32, (RHS, BLK), 1)
    wide = jnp.zeros((RHS, BLK), F32)
    for at, dot in enumerate(dots):
        wide = jnp.where(lane == at, total(dot), wide)
    tall = jnp.concatenate([wide, jnp.zeros((BLK - RHS, BLK), F32)], axis=0).T
    row = tall[0:1]
    for at in range(1, 4):
        row = row + pltpu.roll(tall[at : at + 1], at * RHS, 1)
    dots_ref[...] = jnp.broadcast_to(row, (8, BLK))


def settle(aux, arrived, targets, first):
    return pl.pallas_call(
        settle_kernel,
        in_specs=[VMEM] * 4,
        out_specs=[VMEM] * 2,
        out_shape=[jax.ShapeDtypeStruct((RHS, BLK), F32), jax.ShapeDtypeStruct((8, BLK), F32)],
        compiler_params=PARAMS,
        name="settle",
    )(aux, arrived, targets, first)


def finish_kernel(sums, targets, first_ref, second_ref, solution_ref, residual_ref):
    row = jnp.broadcast_to(jnp.sum(sums[...], axis=0), (8, BLK))
    sub = lax.broadcasted_iota(jnp.int32, (8, BLK), 0)
    rows = jnp.zeros((8, BLK), F32)
    for at in range(4):
        rows = jnp.where(sub == at, pltpu.roll(row, (BLK - at * RHS) % BLK, 1), rows)
    tall = jnp.concatenate([rows, jnp.zeros((BLK - 8, BLK), F32)], axis=0).T
    norm, curve, square, cubic = [tall[:RHS, at : at + 1] for at in range(4)]
    vectors, first = targets[...], first_ref[...]
    step = norm / curve
    norm_next = norm - 2.0 * step * curve + step * step * square
    more = 1.0 + norm_next / norm
    new_curve = more * more * curve - 2.0 * step * more * square + step * step * cubic
    new_step = norm_next / new_curve
    solution_ref[...] = step * vectors + new_step * (more * vectors - step * first)
    residual_ref[...] = vectors - step * first - new_step * (more * first - step * second_ref[...])


def finish(sums, targets, first, second_image):
    shape = jax.ShapeDtypeStruct((RHS, BLK), F32)
    return pl.pallas_call(
        finish_kernel,
        in_specs=[VMEM] * 4,
        out_specs=[VMEM] * 2,
        out_shape=[shape, shape],
        compiler_params=PARAMS,
        name="finish",
    )(sums, targets, first, second_image)


def to_each(x, axes):
    peers = lax.axis_size(axes)
    return exchange(jnp.broadcast_to(x[None], (peers, *x.shape)), axes)


def on_device(points, targets, lengthscales, outputscale, noise):
    near, own, aux = spread(points, lengthscales[None], targets, outputscale, noise)
    near = exchange(near, "y")
    behind, ahead = shift(near, "x", 1), shift(near, "x", -1)
    across = shift(near, "x", 2)
    prepared = own_cols(near)
    below, above, far = shift(own, "z", 1), shift(own, "z", -1), shift(own, "z", 4)
    pairs = [shift(jnp.stack([below, own]), "z", 2), shift(jnp.stack([own, above]), "z", -2)]
    same = jnp.concatenate([jnp.stack([own, below, above, far]), *pairs])
    other = shift(same, "c", 1)
    pieces, high, low, left, left_sq = own_chunk(same, other, prepared)
    highs, lows = [high], [low]
    for cols in (behind, ahead):
        pieces, high, low = more_chunk(ALL, cols, left, left_sq, pieces)
        highs.append(high)
        lows.append(low)
    theirs, high_theirs, low_theirs = more_chunk(THEIRS, across, left, left_sq, pieces)
    theirs = shift(theirs, "c", 1)
    mine, high_mine, low_mine = more_chunk(MINE, across, left, left_sq, pieces)
    arrived = exchange(mine + theirs, "z")
    first, wide = between(aux, arrived, targets)
    gathered = exchange(wide, ("x", "y"))
    theirs = shift(second(THEIRS, gathered, highs + [high_theirs], lows + [low_theirs]), "c", 1)
    mine = second(MINE, gathered, highs + [high_mine], lows + [low_mine])
    arrived = exchange(mine + theirs, "z")
    second_image, dots = settle(aux, arrived, targets, first)
    sums = jnp.sum(to_each(dots[0:1], ("y", "c")), axis=0)
    return tuple(finish(to_each(sums, ("x", "z")), targets, first, second_image))


def solution(mesh):
    finer = Mesh(mesh.devices.reshape(4, 8, 2, mesh.shape["row"]), AXES)
    spec = P(None, AXES)

    return jax.shard_map(
        on_device, mesh=finer, in_specs=(spec, spec, P(), P(), P()), out_specs=(spec, spec), check_vma=False
    )
```

```python
import functools
import math

import jax
import jax.numpy as jnp
from jax import lax
from jax.experimental import pallas as pl
from jax.experimental.pallas import tpu as pltpu
from jax.sharding import Mesh
from jax.sharding import PartitionSpec as P


AXES = ("x", "y", "c", "z")
F32 = jnp.float32
BF16 = jnp.bfloat16
ROOT = math.sqrt(math.log2(math.e))
BLK = 128
RHS = 32
TILE = 512
SUB = 256
WIDE = 1024
VMEM = pl.BlockSpec(memory_space=pltpu.VMEM)
SMEM = pl.BlockSpec(memory_space=pltpu.SMEM)
PARAMS = pltpu.CompilerParams(vmem_limit_bytes=12 << 20)


def shift(value, axis, steps):
    count = lax.axis_size(axis)
    return lax.ppermute(value, axis, [(s, (s + steps) % count) for s in range(count)])


def exchange(x, axes):
    return lax.all_to_all(x, axes, 0, 0, tiled=True)


def halves(x):
    high = x.astype(BF16)
    return high, (x - high.astype(F32)).astype(BF16)


def kept(x):
    return pltpu.with_memory_space_constraint(x, pltpu.VMEM)


def cost(flops=0, moved=0, powers=0):
    return pl.CostEstimate(flops=flops, bytes_accessed=moved, transcendentals=powers)


def spread_kernel(points_in, lengths_in, targets_in, scale, noise, out, own, aux, points, lengths, targets, sems):
    copies = [
        pltpu.make_async_copy(source, to, sems.at[at])
        for at, (source, to) in enumerate(((points_in, points), (lengths_in, lengths), (targets_in, targets)))
    ]
    for copy in copies:
        copy.start()
    for copy in copies:
        copy.wait()
    scaled = points[...] / jnp.broadcast_to(lengths[...], (BLK, BLK)).T
    vectors = targets[...]
    own[...] = scaled
    for peer in range(8):
        out[peer, pl.ds(0, BLK), :] = scaled
        out[peer, pl.ds(BLK, RHS), :] = vectors
    aux[...] = jnp.where(lax.broadcasted_iota(jnp.int32, (8, BLK), 0) == 0, scale[0], noise[0])


def spread(points, lengths, targets, scale, noise):
    return pl.pallas_call(
        spread_kernel,
        in_specs=[pl.BlockSpec(memory_space=pltpu.HBM)] * 3 + [SMEM, SMEM],
        out_specs=[VMEM] * 3,
        scratch_shapes=[
            pltpu.VMEM((BLK, BLK), F32),
            pltpu.VMEM((1, BLK), F32),
            pltpu.VMEM((RHS, BLK), F32),
            pltpu.SemaphoreType.DMA((3,)),
        ],
        out_shape=[
            jax.ShapeDtypeStruct((8, BLK + RHS, BLK), F32),
            jax.ShapeDtypeStruct((BLK, BLK), F32),
            jax.ShapeDtypeStruct((8, BLK), F32),
        ],
        compiler_params=PARAMS,
        name="spread",
    )(*[pltpu.with_memory_space_constraint(v, pltpu.HBM) for v in (points, lengths, targets)], scale, noise)


ORDER = (0, 3, -3, 4, 2, -2, 1, -1)


def prepare_rows(row_refs, left, left_sq):
    place = lax.axis_index("z")
    for block in range(16):
        value = row_refs[block // 8][block % 8] * ROOT
        high, low = halves(value)
        z = lax.rem(place + (ORDER[block % 8] + 8), 8)
        at = block // 8 * 2 + lax.div(z, 4)
        lanes = pl.ds(pl.multiple_of(lax.rem(z, 4) * BLK, BLK), BLK)
        left[at, pl.ds(0, 128), lanes] = high
        left[at, pl.ds(128, 128), lanes] = low
        left[at, pl.ds(256, 128), lanes] = high
        left[at, pl.ds(384, 128), lanes] = low
        left_sq[at, :, lanes] = -0.5 * jnp.sum(value * value, axis=0, keepdims=True)


def prepare_cols(col_refs, right, right_sq, vecs):
    each = 8 // len(col_refs)
    for block in range(8):
        ref, at = col_refs[block // each], block % each
        value = ref[at, pl.ds(0, BLK), :].T * ROOT
        high, low = halves(value)
        rows = pl.ds(block * BLK, BLK)
        right[rows, pl.ds(0, 128)] = high
        right[rows, pl.ds(128, 128)] = high
        right[rows, pl.ds(256, 128)] = low
        right[rows, pl.ds(384, 128)] = low
        right_sq[rows, :] = -0.5 * jnp.sum(value * value, axis=1, keepdims=True)
        high, low = halves(ref[at, pl.ds(BLK, RHS), :])
        vecs[pl.ds(0, RHS), rows] = high
        vecs[pl.ds(RHS, RHS), rows] = low


def make_values(tiles, left, left_sq, right, right_sq, vecs, high_ref, low_ref, out, before):
    def one(to, carry):
        tile = tiles[0] + to
        for step in range(WIDE // SUB):
            rows = pl.ds(step * SUB, SUB)
            power = jnp.dot(right[rows, :], left[tile], preferred_element_type=F32)
            high, low = halves(jnp.exp2(power + right_sq[rows, :] + left_sq[tile]))
            high_ref[to, rows, :] = high
            low_ref[to, rows, :] = low
        both = jnp.dot(vecs[...], high_ref[to], preferred_element_type=F32)
        rest = jnp.dot(vecs[pl.ds(0, RHS), :], low_ref[to], preferred_element_type=F32)
        total = both[:RHS] + both[RHS:] + rest
        for local in range(TILE // BLK):
            piece = total[:, local * BLK : (local + 1) * BLK]
            if before is not None:
                piece = piece + before[tile * (TILE // BLK) + local]
            out[to * (TILE // BLK) + local] = piece
        return carry

    lax.fori_loop(0, len(tiles), one, 0)


def cols_kernel(cols, right, right_sq, vecs):
    prepare_cols((cols,), right, right_sq, vecs)


def own_kernel(same, other, right, right_sq, vecs, out, high, low, left, left_sq):
    prepare_rows((same, other), left, left_sq)
    make_values(ALL, left, left_sq, right, right_sq, vecs, high, low, out, None)


def more_kernel(tiles, cols, left, left_sq, before, out, high, low, right, right_sq, vecs):
    prepare_cols((cols,), right, right_sq, vecs)
    make_values(tiles, left, left_sq, right, right_sq, vecs, high, low, out, before)


ALL, MINE, THEIRS = (0, 1, 2, 3), (0, 1), (2, 3)


def made(tiles):
    values = pltpu.VMEM((len(tiles), WIDE, TILE), BF16)
    return [pltpu.VMEM((len(tiles) * TILE // BLK, RHS, BLK), F32), values, values]


def made_cost(tiles):
    width = len(tiles) * TILE
    return cost(2 * width * WIDE * 768, 4 * width * WIDE, width * WIDE)


LEFT = [pltpu.VMEM((4, 512, TILE), BF16), pltpu.VMEM((4, 1, TILE), F32)]
RIGHT = [pltpu.VMEM((WIDE, 512), BF16), pltpu.VMEM((WIDE, 1), F32), pltpu.VMEM((2 * RHS, WIDE), BF16)]


def own_cols(cols):
    return pl.pallas_call(
        cols_kernel,
        in_specs=[VMEM],
        out_specs=[VMEM] * 3,
        out_shape=RIGHT,
        compiler_params=PARAMS,
        cost_estimate=cost(0, 2 << 20, 0),
        name="own_cols",
    )(cols)


def own_chunk(same, other, cols):
    return pl.pallas_call(
        own_kernel,
        in_specs=[VMEM] * 5,
        out_specs=[VMEM] * 5,
        out_shape=[*made(ALL), *LEFT],
        compiler_params=PARAMS,
        cost_estimate=made_cost(ALL),
        name="own_chunk",
    )(same, other, *[kept(v) for v in cols])


def more_chunk(tiles, cols, left, left_sq, before):
    return pl.pallas_call(
        functools.partial(more_kernel, tiles),
        in_specs=[VMEM] * 4,
        out_specs=[VMEM] * 3,
        out_shape=made(tiles),
        scratch_shapes=RIGHT,
        compiler_params=PARAMS,
        cost_estimate=made_cost(tiles),
    )(cols, kept(left), kept(left_sq), kept(before))


def total(x):
    return jnp.sum(x, axis=1, keepdims=True)


def between_kernel(aux, arrived, targets, first_ref, wide_ref):
    first = aux[0:1, 0:1] * jnp.sum(arrived[...], axis=0) + aux[1:2, 0:1] * targets[...]
    first_ref[...] = first
    for peer in range(32):
        wide_ref[peer] = first


def between(aux, arrived, targets):
    return pl.pallas_call(
        between_kernel,
        in_specs=[VMEM] * 3,
        out_specs=[VMEM] * 2,
        out_shape=[jax.ShapeDtypeStruct((RHS, BLK), F32), jax.ShapeDtypeStruct((32, RHS, BLK), F32)],
        compiler_params=PARAMS,
        name="between",
    )(aux, arrived, targets)


def second_kernel(tiles, gathered, *refs):
    highs, lows, out, vecs = refs[0:4], refs[4:8], refs[8], refs[9]
    place = lax.axis_index("x")
    for chunk in range(4):
        source = lax.rem(place + (0, 3, 1, 2)[chunk], 4) * 8
        for y in range(8):
            lanes = pl.ds(y * BLK, BLK)
            high, low = halves(gathered[source + y])
            vecs[chunk, pl.ds(0, RHS), lanes] = high
            vecs[chunk, pl.ds(RHS, RHS), lanes] = low
    for to, tile in enumerate(tiles):
        product = jnp.zeros((RHS, TILE), F32)
        for chunk in range(4):
            at = to if chunk == 3 else tile
            both = jnp.dot(vecs[chunk], highs[chunk][at], preferred_element_type=F32)
            rest = jnp.dot(vecs[chunk, pl.ds(0, RHS), :], lows[chunk][at], preferred_element_type=F32)
            product = product + both[:RHS] + both[RHS:] + rest
        for local in range(TILE // BLK):
            out[to * (TILE // BLK) + local] = product[:, local * BLK : (local + 1) * BLK]


def second(tiles, gathered, highs, lows):
    width = len(tiles) * TILE
    return pl.pallas_call(
        functools.partial(second_kernel, tiles),
        in_specs=[VMEM] * 9,
        out_specs=VMEM,
        out_shape=pltpu.VMEM((width // BLK, RHS, BLK), F32),
        scratch_shapes=[pltpu.VMEM((4, 2 * RHS, WIDE), BF16)],
        compiler_params=PARAMS,
        cost_estimate=cost(2 * width * 4 * WIDE * 128, 4 * width * 4 * WIDE, 0),
    )(gathered, *[kept(v) for v in highs], *[kept(v) for v in lows])


def total(x):
    return jnp.sum(x, axis=1, keepdims=True)


def settle_kernel(aux, arrived, targets, first_ref, second_ref, dots_ref):
    vectors, first = targets[...], first_ref[...]
    second_image = aux[0:1, 0:1] * jnp.sum(arrived[...], axis=0) + aux[1:2, 0:1] * first
    second_ref[...] = second_image
    dots = (vectors * vectors, vectors * first, first * first, first * second_image)
    lane = lax.broadcasted_iota(jnp.int32, (RHS, BLK), 1)
    wide = jnp.zeros((RHS, BLK), F32)
    for at, dot in enumerate(dots):
        wide = jnp.where(lane == at, total(dot), wide)
    tall = jnp.concatenate([wide, jnp.zeros((BLK - RHS, BLK), F32)], axis=0).T
    row = tall[0:1]
    for at in range(1, 4):
        row = row + pltpu.roll(tall[at : at + 1], at * RHS, 1)
    dots_ref[...] = jnp.broadcast_to(row, (8, BLK))


def settle(aux, arrived, targets, first):
    return pl.pallas_call(
        settle_kernel,
        in_specs=[VMEM] * 4,
        out_specs=[VMEM] * 2,
        out_shape=[jax.ShapeDtypeStruct((RHS, BLK), F32), jax.ShapeDtypeStruct((8, BLK), F32)],
        compiler_params=PARAMS,
        name="settle",
    )(aux, arrived, targets, first)


def finish_kernel(sums, targets, first_ref, second_ref, solution_ref, residual_ref):
    row = jnp.broadcast_to(jnp.sum(sums[...], axis=0), (8, BLK))
    sub = lax.broadcasted_iota(jnp.int32, (8, BLK), 0)
    rows = jnp.zeros((8, BLK), F32)
    for at in range(4):
        rows = jnp.where(sub == at, pltpu.roll(row, (BLK - at * RHS) % BLK, 1), rows)
    tall = jnp.concatenate([rows, jnp.zeros((BLK - 8, BLK), F32)], axis=0).T
    norm, curve, square, cubic = [tall[:RHS, at : at + 1] for at in range(4)]
    vectors, first = targets[...], first_ref[...]
    step = norm / curve
    norm_next = norm - 2.0 * step * curve + step * step * square
    more = 1.0 + norm_next / norm
    new_curve = more * more * curve - 2.0 * step * more * square + step * step * cubic
    new_step = norm_next / new_curve
    solution_ref[...] = step * vectors + new_step * (more * vectors - step * first)
    residual_ref[...] = vectors - step * first - new_step * (more * first - step * second_ref[...])


def finish(sums, targets, first, second_image):
    shape = jax.ShapeDtypeStruct((RHS, BLK), F32)
    return pl.pallas_call(
        finish_kernel,
        in_specs=[VMEM] * 4,
        out_specs=[VMEM] * 2,
        out_shape=[shape, shape],
        compiler_params=PARAMS,
        name="finish",
    )(sums, targets, first, second_image)


def to_each(x, axes):
    peers = lax.axis_size(axes)
    return exchange(jnp.broadcast_to(x[None], (peers, *x.shape)), axes)


def on_device(points, targets, lengthscales, outputscale, noise):
    near, own, aux = spread(points, lengthscales[None], targets, outputscale, noise)
    near = exchange(near, "y")
    behind, ahead = shift(near, "x", 1), shift(near, "x", -1)
    across = shift(near, "x", 2)
    others = [shift(own, "z", -steps) for steps in ORDER[1:]]
    same = jnp.stack([own, *others])
    other = shift(same, "c", 1)
    prepared = own_cols(near)
    pieces, high, low, left, left_sq = own_chunk(same, other, prepared)
    highs, lows = [high], [low]
    for cols in (behind, ahead):
        pieces, high, low = more_chunk(ALL, cols, left, left_sq, pieces)
        highs.append(high)
        lows.append(low)
    theirs, high_theirs, low_theirs = more_chunk(THEIRS, across, left, left_sq, pieces)
    theirs = shift(theirs, "c", 1)
    mine, high_mine, low_mine = more_chunk(MINE, across, left, left_sq, pieces)
    arrived = exchange(mine + theirs, "z")
    first, wide = between(aux, arrived, targets)
    gathered = exchange(wide, ("x", "y"))
    theirs = shift(second(THEIRS, gathered, highs + [high_theirs], lows + [low_theirs]), "c", 1)
    mine = second(MINE, gathered, highs + [high_mine], lows + [low_mine])
    arrived = exchange(mine + theirs, "z")
    second_image, dots = settle(aux, arrived, targets, first)
    sums = jnp.sum(to_each(dots[0:1], ("y", "c")), axis=0)
    return tuple(finish(to_each(sums, ("x", "z")), targets, first, second_image))


def solution(mesh):
    finer = Mesh(mesh.devices.reshape(4, 8, 2, mesh.shape["row"]), AXES)
    spec = P(None, AXES)

    return jax.shard_map(
        on_device, mesh=finer, in_specs=(spec, spec, P(), P(), P()), out_specs=(spec, spec), check_vma=False
    )
```

```python
import functools
import math

import jax
import jax.numpy as jnp
from jax import lax
from jax.experimental import pallas as pl
from jax.experimental.pallas import tpu as pltpu
from jax.sharding import Mesh
from jax.sharding import PartitionSpec as P


AXES = ("x", "y", "c", "z")
F32 = jnp.float32
BF16 = jnp.bfloat16
ROOT = math.sqrt(math.log2(math.e))
BLK = 128
RHS = 32
TILE = 512
SUB = 256
WIDE = 1024
VMEM = pl.BlockSpec(memory_space=pltpu.VMEM)
SMEM = pl.BlockSpec(memory_space=pltpu.SMEM)
PARAMS = pltpu.CompilerParams(vmem_limit_bytes=12 << 20)


def shift(value, axis, steps):
    count = lax.axis_size(axis)
    return lax.ppermute(value, axis, [(s, (s + steps) % count) for s in range(count)])


def exchange(x, axes):
    return lax.all_to_all(x, axes, 0, 0, tiled=True)


def halves(x):
    high = x.astype(BF16)
    return high, (x - high.astype(F32)).astype(BF16)


def kept(x):
    return pltpu.with_memory_space_constraint(x, pltpu.VMEM)


def cost(flops=0, moved=0, powers=0):
    return pl.CostEstimate(flops=flops, bytes_accessed=moved, transcendentals=powers)


def spread_kernel(points_in, lengths_in, targets_in, scale, noise, out, own, aux, points, lengths, targets, sems):
    copies = [
        pltpu.make_async_copy(source, to, sems.at[at])
        for at, (source, to) in enumerate(((points_in, points), (lengths_in, lengths), (targets_in, targets)))
    ]
    for copy in copies:
        copy.start()
    for copy in copies:
        copy.wait()
    scaled = points[...] / jnp.broadcast_to(lengths[...], (BLK, BLK)).T
    vectors = targets[...]
    own[...] = scaled
    for peer in range(8):
        out[peer, pl.ds(0, BLK), :] = scaled
        out[peer, pl.ds(BLK, RHS), :] = vectors
    aux[...] = jnp.where(lax.broadcasted_iota(jnp.int32, (8, BLK), 0) == 0, scale[0], noise[0])


def spread(points, lengths, targets, scale, noise):
    return pl.pallas_call(
        spread_kernel,
        in_specs=[pl.BlockSpec(memory_space=pltpu.HBM)] * 3 + [SMEM, SMEM],
        out_specs=[VMEM] * 3,
        scratch_shapes=[
            pltpu.VMEM((BLK, BLK), F32),
            pltpu.VMEM((1, BLK), F32),
            pltpu.VMEM((RHS, BLK), F32),
            pltpu.SemaphoreType.DMA((3,)),
        ],
        out_shape=[
            jax.ShapeDtypeStruct((8, BLK + RHS, BLK), F32),
            jax.ShapeDtypeStruct((BLK, BLK), F32),
            jax.ShapeDtypeStruct((8, BLK), F32),
        ],
        compiler_params=PARAMS,
        name="spread",
    )(*[pltpu.with_memory_space_constraint(v, pltpu.HBM) for v in (points, lengths, targets)], scale, noise)


ORDER = (0, -1, 1, 4, -3, -2, 2, 3)


def prepare_rows(row_refs, left, left_sq):
    place = lax.axis_index("z")
    for block in range(16):
        value = row_refs[block // 8][block % 8] * ROOT
        high, low = halves(value)
        z = lax.rem(place + (ORDER[block % 8] + 8), 8)
        at = block // 8 * 2 + lax.div(z, 4)
        lanes = pl.ds(pl.multiple_of(lax.rem(z, 4) * BLK, BLK), BLK)
        left[at, pl.ds(0, 128), lanes] = high
        left[at, pl.ds(128, 128), lanes] = low
        left[at, pl.ds(256, 128), lanes] = high
        left[at, pl.ds(384, 128), lanes] = low
        left_sq[at, :, lanes] = -0.5 * jnp.sum(value * value, axis=0, keepdims=True)


def prepare_cols(col_refs, right, right_sq, vecs):
    each = 8 // len(col_refs)
    for block in range(8):
        ref, at = col_refs[block // each], block % each
        value = ref[at, pl.ds(0, BLK), :].T * ROOT
        high, low = halves(value)
        rows = pl.ds(block * BLK, BLK)
        right[rows, pl.ds(0, 128)] = high
        right[rows, pl.ds(128, 128)] = high
        right[rows, pl.ds(256, 128)] = low
        right[rows, pl.ds(384, 128)] = low
        right_sq[rows, :] = -0.5 * jnp.sum(value * value, axis=1, keepdims=True)
        high, low = halves(ref[at, pl.ds(BLK, RHS), :])
        vecs[pl.ds(0, RHS), rows] = high
        vecs[pl.ds(RHS, RHS), rows] = low


def make_values(tiles, left, left_sq, right, right_sq, vecs, high_ref, low_ref, out, before):
    def one(to, carry):
        tile = tiles[0] + to
        for step in range(WIDE // SUB):
            rows = pl.ds(step * SUB, SUB)
            power = jnp.dot(right[rows, :], left[tile], preferred_element_type=F32)
            high, low = halves(jnp.exp2(power + right_sq[rows, :] + left_sq[tile]))
            high_ref[to, rows, :] = high
            low_ref[to, rows, :] = low
        both = jnp.dot(vecs[...], high_ref[to], preferred_element_type=F32)
        rest = jnp.dot(vecs[pl.ds(0, RHS), :], low_ref[to], preferred_element_type=F32)
        total = both[:RHS] + both[RHS:] + rest
        for local in range(TILE // BLK):
            piece = total[:, local * BLK : (local + 1) * BLK]
            if before is not None:
                piece = piece + before[tile * (TILE // BLK) + local]
            out[to * (TILE // BLK) + local] = piece
        return carry

    lax.fori_loop(0, len(tiles), one, 0)


def cols_kernel(cols, right, right_sq, vecs):
    prepare_cols((cols,), right, right_sq, vecs)


def own_kernel(same, other, right, right_sq, vecs, out, high, low, left, left_sq):
    prepare_rows((same, other), left, left_sq)
    make_values(ALL, left, left_sq, right, right_sq, vecs, high, low, out, None)


def more_kernel(tiles, cols, left, left_sq, before, out, high, low, right, right_sq, vecs):
    prepare_cols((cols,), right, right_sq, vecs)
    make_values(tiles, left, left_sq, right, right_sq, vecs, high, low, out, before)


ALL, MINE, THEIRS = (0, 1, 2, 3), (0, 1), (2, 3)


def made(tiles):
    values = pltpu.VMEM((len(tiles), WIDE, TILE), BF16)
    return [pltpu.VMEM((len(tiles) * TILE // BLK, RHS, BLK), F32), values, values]


def made_cost(tiles):
    width = len(tiles) * TILE
    return cost(2 * width * WIDE * 768, 4 * width * WIDE, width * WIDE)


LEFT = [pltpu.VMEM((4, 512, TILE), BF16), pltpu.VMEM((4, 1, TILE), F32)]
RIGHT = [pltpu.VMEM((WIDE, 512), BF16), pltpu.VMEM((WIDE, 1), F32), pltpu.VMEM((2 * RHS, WIDE), BF16)]


def own_cols(cols):
    return pl.pallas_call(
        cols_kernel,
        in_specs=[VMEM],
        out_specs=[VMEM] * 3,
        out_shape=RIGHT,
        compiler_params=PARAMS,
        cost_estimate=cost(0, 2 << 20, 0),
        name="own_cols",
    )(cols)


def own_chunk(same, other, cols):
    return pl.pallas_call(
        own_kernel,
        in_specs=[VMEM] * 5,
        out_specs=[VMEM] * 5,
        out_shape=[*made(ALL), *LEFT],
        compiler_params=PARAMS,
        cost_estimate=made_cost(ALL),
        name="own_chunk",
    )(same, other, *[kept(v) for v in cols])


def more_chunk(tiles, cols, left, left_sq, before):
    return pl.pallas_call(
        functools.partial(more_kernel, tiles),
        in_specs=[VMEM] * 4,
        out_specs=[VMEM] * 3,
        out_shape=made(tiles),
        scratch_shapes=RIGHT,
        compiler_params=PARAMS,
        cost_estimate=made_cost(tiles),
    )(cols, kept(left), kept(left_sq), kept(before))


def total(x):
    return jnp.sum(x, axis=1, keepdims=True)


def between_kernel(aux, arrived, targets, first_ref, wide_ref):
    first = aux[0:1, 0:1] * jnp.sum(arrived[...], axis=0) + aux[1:2, 0:1] * targets[...]
    first_ref[...] = first
    for peer in range(32):
        wide_ref[peer] = first


def between(aux, arrived, targets):
    return pl.pallas_call(
        between_kernel,
        in_specs=[VMEM] * 3,
        out_specs=[VMEM] * 2,
        out_shape=[jax.ShapeDtypeStruct((RHS, BLK), F32), jax.ShapeDtypeStruct((32, RHS, BLK), F32)],
        compiler_params=PARAMS,
        name="between",
    )(aux, arrived, targets)


def second_kernel(tiles, gathered, *refs):
    highs, lows, out, vecs = refs[0:4], refs[4:8], refs[8], refs[9]
    place = lax.axis_index("x")
    for chunk in range(4):
        source = lax.rem(place + (0, 3, 1, 2)[chunk], 4) * 8
        for y in range(8):
            lanes = pl.ds(y * BLK, BLK)
            high, low = halves(gathered[source + y])
            vecs[chunk, pl.ds(0, RHS), lanes] = high
            vecs[chunk, pl.ds(RHS, RHS), lanes] = low
    for to, tile in enumerate(tiles):
        product = jnp.zeros((RHS, TILE), F32)
        for chunk in range(4):
            at = to if chunk == 3 else tile
            both = jnp.dot(vecs[chunk], highs[chunk][at], preferred_element_type=F32)
            rest = jnp.dot(vecs[chunk, pl.ds(0, RHS), :], lows[chunk][at], preferred_element_type=F32)
            product = product + both[:RHS] + both[RHS:] + rest
        for local in range(TILE // BLK):
            out[to * (TILE // BLK) + local] = product[:, local * BLK : (local + 1) * BLK]


def second(tiles, gathered, highs, lows):
    width = len(tiles) * TILE
    return pl.pallas_call(
        functools.partial(second_kernel, tiles),
        in_specs=[VMEM] * 9,
        out_specs=VMEM,
        out_shape=pltpu.VMEM((width // BLK, RHS, BLK), F32),
        scratch_shapes=[pltpu.VMEM((4, 2 * RHS, WIDE), BF16)],
        compiler_params=PARAMS,
        cost_estimate=cost(2 * width * 4 * WIDE * 128, 4 * width * 4 * WIDE, 0),
    )(gathered, *[kept(v) for v in highs], *[kept(v) for v in lows])


def total(x):
    return jnp.sum(x, axis=1, keepdims=True)


def settle_kernel(aux, arrived, targets, first_ref, second_ref, dots_ref):
    vectors, first = targets[...], first_ref[...]
    second_image = aux[0:1, 0:1] * jnp.sum(arrived[...], axis=0) + aux[1:2, 0:1] * first
    second_ref[...] = second_image
    dots = (vectors * vectors, vectors * first, first * first, first * second_image)
    lane = lax.broadcasted_iota(jnp.int32, (RHS, BLK), 1)
    wide = jnp.zeros((RHS, BLK), F32)
    for at, dot in enumerate(dots):
        wide = jnp.where(lane == at, total(dot), wide)
    tall = jnp.concatenate([wide, jnp.zeros((BLK - RHS, BLK), F32)], axis=0).T
    row = tall[0:1]
    for at in range(1, 4):
        row = row + pltpu.roll(tall[at : at + 1], at * RHS, 1)
    dots_ref[...] = jnp.broadcast_to(row, (8, BLK))


def settle(aux, arrived, targets, first):
    return pl.pallas_call(
        settle_kernel,
        in_specs=[VMEM] * 4,
        out_specs=[VMEM] * 2,
        out_shape=[jax.ShapeDtypeStruct((RHS, BLK), F32), jax.ShapeDtypeStruct((8, BLK), F32)],
        compiler_params=PARAMS,
        name="settle",
    )(aux, arrived, targets, first)


def finish_kernel(sums, targets, first_ref, second_ref, solution_ref, residual_ref):
    row = jnp.broadcast_to(jnp.sum(sums[...], axis=0), (8, BLK))
    sub = lax.broadcasted_iota(jnp.int32, (8, BLK), 0)
    rows = jnp.zeros((8, BLK), F32)
    for at in range(4):
        rows = jnp.where(sub == at, pltpu.roll(row, (BLK - at * RHS) % BLK, 1), rows)
    tall = jnp.concatenate([rows, jnp.zeros((BLK - 8, BLK), F32)], axis=0).T
    norm, curve, square, cubic = [tall[:RHS, at : at + 1] for at in range(4)]
    vectors, first = targets[...], first_ref[...]
    step = norm / curve
    norm_next = norm - 2.0 * step * curve + step * step * square
    more = 1.0 + norm_next / norm
    new_curve = more * more * curve - 2.0 * step * more * square + step * step * cubic
    new_step = norm_next / new_curve
    solution_ref[...] = step * vectors + new_step * (more * vectors - step * first)
    residual_ref[...] = vectors - step * first - new_step * (more * first - step * second_ref[...])


def finish(sums, targets, first, second_image):
    shape = jax.ShapeDtypeStruct((RHS, BLK), F32)
    return pl.pallas_call(
        finish_kernel,
        in_specs=[VMEM] * 4,
        out_specs=[VMEM] * 2,
        out_shape=[shape, shape],
        compiler_params=PARAMS,
        name="finish",
    )(sums, targets, first, second_image)


def to_each(x, axes):
    peers = lax.axis_size(axes)
    return exchange(jnp.broadcast_to(x[None], (peers, *x.shape)), axes)


def on_device(points, targets, lengthscales, outputscale, noise):
    near, own, aux = spread(points, lengthscales[None], targets, outputscale, noise)
    near = exchange(near, "y")
    behind, ahead = shift(near, "x", 1), shift(near, "x", -1)
    across = shift(near, "x", 2)
    below, above, far = shift(own, "z", 1), shift(own, "z", -1), shift(own, "z", 4)
    pairs = [shift(jnp.stack([below, own]), "z", 2), shift(jnp.stack([own, above]), "z", -2)]
    same = jnp.concatenate([jnp.stack([own, below, above, far]), *pairs])
    other = shift(same, "c", 1)
    prepared = own_cols(near)
    pieces, high, low, left, left_sq = own_chunk(same, other, prepared)
    highs, lows = [high], [low]
    for cols in (behind, ahead):
        pieces, high, low = more_chunk(ALL, cols, left, left_sq, pieces)
        highs.append(high)
        lows.append(low)
    theirs, high_theirs, low_theirs = more_chunk(THEIRS, across, left, left_sq, pieces)
    theirs = shift(theirs, "c", 1)
    mine, high_mine, low_mine = more_chunk(MINE, across, left, left_sq, pieces)
    arrived = exchange(mine + theirs, "z")
    first, wide = between(aux, arrived, targets)
    gathered = exchange(wide, ("x", "y"))
    theirs = shift(second(THEIRS, gathered, highs + [high_theirs], lows + [low_theirs]), "c", 1)
    mine = second(MINE, gathered, highs + [high_mine], lows + [low_mine])
    arrived = exchange(mine + theirs, "z")
    second_image, dots = settle(aux, arrived, targets, first)
    sums = jnp.sum(to_each(dots[0:1], ("y", "c")), axis=0)
    return tuple(finish(to_each(sums, ("x", "z")), targets, first, second_image))


def solution(mesh):
    finer = Mesh(mesh.devices.reshape(4, 8, 2, mesh.shape["row"]), AXES)
    spec = P(None, AXES)

    return jax.shard_map(
        on_device, mesh=finer, in_specs=(spec, spec, P(), P(), P()), out_specs=(spec, spec), check_vma=False
    )
```

```python
import functools
import math

import jax
import jax.numpy as jnp
from jax import lax
from jax.experimental import pallas as pl
from jax.experimental.pallas import tpu as pltpu
from jax.sharding import Mesh
from jax.sharding import PartitionSpec as P


AXES = ("x", "y", "c", "z")
F32 = jnp.float32
BF16 = jnp.bfloat16
ROOT = math.sqrt(math.log2(math.e))
BLK = 128
RHS = 32
TILE = 512
SUB = 256
WIDE = 1024
VMEM = pl.BlockSpec(memory_space=pltpu.VMEM)
SMEM = pl.BlockSpec(memory_space=pltpu.SMEM)
PARAMS = pltpu.CompilerParams(vmem_limit_bytes=12 << 20)


def shift(value, axis, steps):
    count = lax.axis_size(axis)
    return lax.ppermute(value, axis, [(s, (s + steps) % count) for s in range(count)])


def exchange(x, axes):
    return lax.all_to_all(x, axes, 0, 0, tiled=True)


def halves(x):
    high = x.astype(BF16)
    return high, (x - high.astype(F32)).astype(BF16)


def kept(x):
    return pltpu.with_memory_space_constraint(x, pltpu.VMEM)


def cost(flops=0, moved=0, powers=0):
    return pl.CostEstimate(flops=flops, bytes_accessed=moved, transcendentals=powers)


def spread_kernel(points_in, lengths_in, targets_in, scale, noise, out, own, aux, points, lengths, targets, sems):
    copies = [
        pltpu.make_async_copy(source, to, sems.at[at])
        for at, (source, to) in enumerate(((points_in, points), (lengths_in, lengths), (targets_in, targets)))
    ]
    for copy in copies:
        copy.start()
    for copy in copies:
        copy.wait()
    scaled = points[...] / jnp.broadcast_to(lengths[...], (BLK, BLK)).T
    vectors = targets[...]
    own[...] = scaled
    for peer in range(8):
        out[peer, pl.ds(0, BLK), :] = scaled
        out[peer, pl.ds(BLK, RHS), :] = vectors
    aux[...] = jnp.where(lax.broadcasted_iota(jnp.int32, (8, BLK), 0) == 0, scale[0], noise[0])


def spread(points, lengths, targets, scale, noise):
    return pl.pallas_call(
        spread_kernel,
        in_specs=[pl.BlockSpec(memory_space=pltpu.HBM)] * 3 + [SMEM, SMEM],
        out_specs=[VMEM] * 3,
        scratch_shapes=[
            pltpu.VMEM((BLK, BLK), F32),
            pltpu.VMEM((1, BLK), F32),
            pltpu.VMEM((RHS, BLK), F32),
            pltpu.SemaphoreType.DMA((3,)),
        ],
        out_shape=[
            jax.ShapeDtypeStruct((8, BLK + RHS, BLK), F32),
            jax.ShapeDtypeStruct((BLK, BLK), F32),
            jax.ShapeDtypeStruct((8, BLK), F32),
        ],
        compiler_params=PARAMS,
        name="spread",
    )(*[pltpu.with_memory_space_constraint(v, pltpu.HBM) for v in (points, lengths, targets)], scale, noise)


ORDER = (0, -1, 1, 4, -3, -2, 2, 3)


def prepare_rows(values, left, left_sq):
    for block, value in enumerate(values):
        value = value * ROOT
        high, low = halves(value)
        at, lanes = block * BLK // TILE, pl.ds(block * BLK % TILE, BLK)
        left[at, pl.ds(0, 128), lanes] = high
        left[at, pl.ds(128, 128), lanes] = low
        left[at, pl.ds(256, 128), lanes] = high
        left[at, pl.ds(384, 128), lanes] = low
        left_sq[at, :, lanes] = -0.5 * jnp.sum(value * value, axis=0, keepdims=True)


def place_of(tile, local):
    return lax.rem(lax.axis_index("z") + (ORDER[tile % 2 * 4 + local] + 8), 8)


def prepare_cols(col_refs, right, right_sq, vecs):
    each = 8 // len(col_refs)
    for block in range(8):
        ref, at = col_refs[block // each], block % each
        value = ref[at, pl.ds(0, BLK), :].T * ROOT
        high, low = halves(value)
        rows = pl.ds(block * BLK, BLK)
        right[rows, pl.ds(0, 128)] = high
        right[rows, pl.ds(128, 128)] = high
        right[rows, pl.ds(256, 128)] = low
        right[rows, pl.ds(384, 128)] = low
        right_sq[rows, :] = -0.5 * jnp.sum(value * value, axis=1, keepdims=True)
        high, low = halves(ref[at, pl.ds(BLK, RHS), :])
        vecs[pl.ds(0, RHS), rows] = high
        vecs[pl.ds(RHS, RHS), rows] = low


def make_values(left, left_sq, right, right_sq, vecs, high, low):
    for step in range(WIDE // SUB):
        rows = pl.ds(step * SUB, SUB)
        power = jnp.dot(right[rows, :], left[...], preferred_element_type=F32)
        high[rows, :], low[rows, :] = halves(jnp.exp2(power + right_sq[rows, :] + left_sq[...]))
    both = jnp.dot(vecs[...], high[...], preferred_element_type=F32)
    rest = jnp.dot(vecs[pl.ds(0, RHS), :], low[...], preferred_element_type=F32)
    product = both[:RHS] + both[RHS:] + rest
    return [product[:, local * BLK : (local + 1) * BLK] for local in range(TILE // BLK)]


def cols_kernel(cols, right, right_sq, vecs):
    prepare_cols((cols,), right, right_sq, vecs)


def own_kernel(count, *refs):
    blocks, (right, right_sq, vecs, out, high, low, left, left_sq) = refs[:count], refs[count:]
    values = []
    for ref in blocks:
        values += [ref[...]] if len(ref.shape) == 2 else [ref[at] for at in range(ref.shape[0])]
    prepare_rows(values, left, left_sq)
    for to in range(len(values) * BLK // TILE):
        made = make_values(left.at[to], left_sq.at[to], right, right_sq, vecs, high.at[to], low.at[to])
        for local, piece in enumerate(made):
            out[to * 4 + local] = piece


def more_kernel(tiles, last, *refs):
    cols, refs = refs[:2], refs[2:]
    lefts, befores, (out, high, low, right, right_sq, vecs) = refs[:6], refs[6:-6], refs[-6:]
    prepare_cols(cols, right, right_sq, vecs)
    for to, tile in enumerate(tiles):
        ref, at = WHERE[tile]
        made = make_values(
            lefts[ref].at[at], lefts[3 + ref].at[at], right, right_sq, vecs, high.at[to], low.at[to]
        )
        for local, piece in enumerate(made):
            before = befores[0][tile * 4 + local] if len(befores) == 1 else befores[ref][at * 4 + local]
            out[place_of(tile, local) if last else to * 4 + local] = piece + before


WHERE = ((0, 0), (1, 0), (2, 0), (2, 1))
ALL, MINE, THEIRS = (0, 1, 2, 3), (0, 1), (2, 3)


def made(tiles):
    values = pltpu.VMEM((len(tiles), WIDE, TILE), BF16)
    return [pltpu.VMEM((len(tiles) * TILE // BLK, RHS, BLK), F32), values, values]


def made_cost(tiles):
    width = len(tiles) * TILE
    return cost(2 * width * WIDE * 768, 4 * width * WIDE, width * WIDE)


RIGHT = [pltpu.VMEM((WIDE, 512), BF16), pltpu.VMEM((WIDE, 1), F32), pltpu.VMEM((2 * RHS, WIDE), BF16)]


def own_cols(cols):
    return pl.pallas_call(
        cols_kernel,
        in_specs=[VMEM],
        out_specs=[VMEM] * 3,
        out_shape=RIGHT,
        compiler_params=PARAMS,
        cost_estimate=cost(0, 2 << 20, 0),
        name="own_cols",
    )(cols)


def own_chunk(blocks, cols, tiles):
    return pl.pallas_call(
        functools.partial(own_kernel, len(blocks)),
        in_specs=[VMEM] * (len(blocks) + 3),
        out_specs=[VMEM] * 5,
        out_shape=[*made(tiles), pltpu.VMEM((len(tiles), 512, TILE), BF16), pltpu.VMEM((len(tiles), 1, TILE), F32)],
        compiler_params=PARAMS,
        cost_estimate=made_cost(tiles),
    )(*blocks, *[kept(v) for v in cols])


def more_chunk(tiles, cols, lefts, befores, last=False):
    return pl.pallas_call(
        functools.partial(more_kernel, tiles, last),
        in_specs=[VMEM] * (8 + len(befores)),
        out_specs=[VMEM] * 3,
        out_shape=made(tiles),
        scratch_shapes=RIGHT,
        compiler_params=PARAMS,
        cost_estimate=made_cost(tiles),
    )(*cols, *[kept(v) for v in lefts], *[kept(v) for v in befores])


def total(x):
    return jnp.sum(x, axis=1, keepdims=True)


def between_kernel(aux, arrived, targets, first_ref, wide_ref):
    first = aux[0:1, 0:1] * jnp.sum(arrived[...], axis=0) + aux[1:2, 0:1] * targets[...]
    first_ref[...] = first
    for peer in range(32):
        wide_ref[peer] = first


def between(aux, arrived, targets):
    return pl.pallas_call(
        between_kernel,
        in_specs=[VMEM] * 3,
        out_specs=[VMEM] * 2,
        out_shape=[jax.ShapeDtypeStruct((RHS, BLK), F32), jax.ShapeDtypeStruct((32, RHS, BLK), F32)],
        compiler_params=PARAMS,
        name="between",
    )(aux, arrived, targets)


def second_kernel(tiles, gathered, *refs):
    highs, lows, out, vecs = refs[0:7], refs[7:14], refs[14], refs[15]
    place = lax.axis_index("x")
    for chunk in range(4):
        source = lax.rem(place + (0, 3, 1, 2)[chunk], 4) * 8
        for y in range(8):
            lanes = pl.ds(y * BLK, BLK)
            high, low = halves(gathered[source + y])
            vecs[chunk, pl.ds(0, RHS), lanes] = high
            vecs[chunk, pl.ds(RHS, RHS), lanes] = low
    for tile in tiles:
        product = jnp.zeros((RHS, TILE), F32)
        for chunk in range(4):
            ref, at = ((0, 1, 2, 2)[tile], (0, 0, 0, 1)[tile]) if chunk == 0 else (2 + chunk, tile)
            if chunk == 3:
                ref, at = 5 + tile // 2, tile % 2
            both = jnp.dot(vecs[chunk], highs[ref][at], preferred_element_type=F32)
            rest = jnp.dot(vecs[chunk, pl.ds(0, RHS), :], lows[ref][at], preferred_element_type=F32)
            product = product + both[:RHS] + both[RHS:] + rest
        for local in range(TILE // BLK):
            out[place_of(tile, local)] = product[:, local * BLK : (local + 1) * BLK]


def second(tiles, gathered, highs, lows):
    width = len(tiles) * TILE
    return pl.pallas_call(
        functools.partial(second_kernel, tiles),
        in_specs=[VMEM] * (1 + len(highs) + len(lows)),
        out_specs=VMEM,
        out_shape=pltpu.VMEM((width // BLK, RHS, BLK), F32),
        scratch_shapes=[pltpu.VMEM((4, 2 * RHS, WIDE), BF16)],
        compiler_params=PARAMS,
        cost_estimate=cost(2 * width * 4 * WIDE * 128, 4 * width * 4 * WIDE, 0),
    )(gathered, *[kept(v) for v in highs], *[kept(v) for v in lows])


def total(x):
    return jnp.sum(x, axis=1, keepdims=True)


def settle_kernel(aux, arrived, targets, first_ref, second_ref, dots_ref):
    vectors, first = targets[...], first_ref[...]
    second_image = aux[0:1, 0:1] * jnp.sum(arrived[...], axis=0) + aux[1:2, 0:1] * first
    second_ref[...] = second_image
    dots = (vectors * vectors, vectors * first, first * first, first * second_image)
    lane = lax.broadcasted_iota(jnp.int32, (RHS, BLK), 1)
    wide = jnp.zeros((RHS, BLK), F32)
    for at, dot in enumerate(dots):
        wide = jnp.where(lane == at, total(dot), wide)
    tall = jnp.concatenate([wide, jnp.zeros((BLK - RHS, BLK), F32)], axis=0).T
    row = tall[0:1]
    for at in range(1, 4):
        row = row + pltpu.roll(tall[at : at + 1], at * RHS, 1)
    dots_ref[...] = jnp.broadcast_to(row, (8, BLK))


def settle(aux, arrived, targets, first):
    return pl.pallas_call(
        settle_kernel,
        in_specs=[VMEM] * 4,
        out_specs=[VMEM] * 2,
        out_shape=[jax.ShapeDtypeStruct((RHS, BLK), F32), jax.ShapeDtypeStruct((8, BLK), F32)],
        compiler_params=PARAMS,
        name="settle",
    )(aux, arrived, targets, first)


def finish_kernel(sums, targets, first_ref, second_ref, solution_ref, residual_ref):
    row = jnp.broadcast_to(jnp.sum(sums[...], axis=0), (8, BLK))
    sub = lax.broadcasted_iota(jnp.int32, (8, BLK), 0)
    rows = jnp.zeros((8, BLK), F32)
    for at in range(4):
        rows = jnp.where(sub == at, pltpu.roll(row, (BLK - at * RHS) % BLK, 1), rows)
    tall = jnp.concatenate([rows, jnp.zeros((BLK - 8, BLK), F32)], axis=0).T
    norm, curve, square, cubic = [tall[:RHS, at : at + 1] for at in range(4)]
    vectors, first = targets[...], first_ref[...]
    step = norm / curve
    norm_next = norm - 2.0 * step * curve + step * step * square
    more = 1.0 + norm_next / norm
    new_curve = more * more * curve - 2.0 * step * more * square + step * step * cubic
    new_step = norm_next / new_curve
    solution_ref[...] = step * vectors + new_step * (more * vectors - step * first)
    residual_ref[...] = vectors - step * first - new_step * (more * first - step * second_ref[...])


def finish(sums, targets, first, second_image):
    shape = jax.ShapeDtypeStruct((RHS, BLK), F32)
    return pl.pallas_call(
        finish_kernel,
        in_specs=[VMEM] * 4,
        out_specs=[VMEM] * 2,
        out_shape=[shape, shape],
        compiler_params=PARAMS,
        name="finish",
    )(sums, targets, first, second_image)


def to_each(x, axes):
    peers = lax.axis_size(axes)
    return exchange(jnp.broadcast_to(x[None], (peers, *x.shape)), axes)


def on_device(points, targets, lengthscales, outputscale, noise):
    near, own, aux = spread(points, lengthscales[None], targets, outputscale, noise)
    near = exchange(near, "y")
    behind_low, ahead_high = shift(near[:4], "x", 1), shift(near[4:], "x", -1)
    behind_high, ahead_low = shift(near[4:], "x", 1), shift(near[:4], "x", -1)
    across = [shift(behind_low, "x", 1), shift(ahead_high, "x", -1)]
    below, above, far = shift(own, "z", 1), shift(own, "z", -1), shift(own, "z", 4)
    pairs = [shift(jnp.stack([below, own]), "z", 2), shift(jnp.stack([own, above]), "z", -2)]
    prepared = own_cols(near)
    chunks = []
    chunks.append(own_chunk([own, below, above, far], prepared, (0,)))
    same = jnp.concatenate([jnp.stack([own, below, above, far]), *pairs])
    other = shift(same, "c", 1)
    chunks.append(own_chunk(pairs, prepared, (1,)))
    chunks.append(own_chunk([other], prepared, THEIRS))
    pieces, highs, lows, left, left_sq = [list(part) for part in zip(*chunks)]
    lefts = [*left, *left_sq]
    for cols in ([behind_low, behind_high], [ahead_low, ahead_high]):
        piece, high, low = more_chunk(ALL, cols, lefts, pieces)
        pieces = [piece]
        highs.append(high)
        lows.append(low)
    theirs, high_theirs, low_theirs = more_chunk(THEIRS, across, lefts, pieces, True)
    theirs = shift(theirs, "c", 1)
    mine, high_mine, low_mine = more_chunk(MINE, across, lefts, pieces, True)
    highs += [high_mine, high_theirs]
    lows += [low_mine, low_theirs]
    arrived = exchange(mine + theirs, "z")
    first, wide = between(aux, arrived, targets)
    gathered = exchange(wide, ("x", "y"))
    theirs = shift(second(THEIRS, gathered, highs, lows), "c", 1)
    mine = second(MINE, gathered, highs, lows)
    arrived = exchange(mine + theirs, "z")
    second_image, dots = settle(aux, arrived, targets, first)
    sums = jnp.sum(to_each(dots[0:1], ("y", "c")), axis=0)
    return tuple(finish(to_each(sums, ("x", "z")), targets, first, second_image))


def solution(mesh):
    finer = Mesh(mesh.devices.reshape(4, 8, 2, mesh.shape["row"]), AXES)
    spec = P(None, AXES)

    return jax.shard_map(
        on_device, mesh=finer, in_specs=(spec, spec, P(), P(), P()), out_specs=(spec, spec), check_vma=False
    )
```

```python
import functools
import math

import jax
import jax.numpy as jnp
from jax import lax
from jax.experimental import pallas as pl
from jax.experimental.pallas import tpu as pltpu
from jax.sharding import Mesh
from jax.sharding import PartitionSpec as P


AXES = ("x", "y", "c", "z")
F32 = jnp.float32
BF16 = jnp.bfloat16
ROOT = math.sqrt(math.log2(math.e))
BLK = 128
RHS = 32
TILE = 512
SUB = 256
WIDE = 1024
VMEM = pl.BlockSpec(memory_space=pltpu.VMEM)
SMEM = pl.BlockSpec(memory_space=pltpu.SMEM)
PARAMS = pltpu.CompilerParams(vmem_limit_bytes=12 << 20)


def shift(value, axis, steps):
    count = lax.axis_size(axis)
    return lax.ppermute(value, axis, [(s, (s + steps) % count) for s in range(count)])


def exchange(x, axes):
    return lax.all_to_all(x, axes, 0, 0, tiled=True)


def halves(x):
    high = x.astype(BF16)
    return high, (x - high.astype(F32)).astype(BF16)


def kept(x):
    return pltpu.with_memory_space_constraint(x, pltpu.VMEM)


def cost(flops=0, moved=0, powers=0):
    return pl.CostEstimate(flops=flops, bytes_accessed=moved, transcendentals=powers)


def spread_kernel(points_in, lengths_in, targets_in, scale, noise, out, own, aux, points, lengths, targets, sems):
    copies = [
        pltpu.make_async_copy(source, to, sems.at[at])
        for at, (source, to) in enumerate(((points_in, points), (lengths_in, lengths), (targets_in, targets)))
    ]
    for copy in copies:
        copy.start()
    for copy in copies:
        copy.wait()
    scaled = points[...] / jnp.broadcast_to(lengths[...], (BLK, BLK)).T
    vectors = targets[...]
    own[...] = scaled
    for peer in range(8):
        out[peer, pl.ds(0, BLK), :] = scaled
        out[peer, pl.ds(BLK, RHS), :] = vectors
    aux[...] = jnp.where(lax.broadcasted_iota(jnp.int32, (8, BLK), 0) == 0, scale[0], noise[0])


def spread(points, lengths, targets, scale, noise):
    return pl.pallas_call(
        spread_kernel,
        in_specs=[pl.BlockSpec(memory_space=pltpu.HBM)] * 3 + [SMEM, SMEM],
        out_specs=[VMEM] * 3,
        scratch_shapes=[
            pltpu.VMEM((BLK, BLK), F32),
            pltpu.VMEM((1, BLK), F32),
            pltpu.VMEM((RHS, BLK), F32),
            pltpu.SemaphoreType.DMA((3,)),
        ],
        out_shape=[
            jax.ShapeDtypeStruct((8, BLK + RHS, BLK), F32),
            jax.ShapeDtypeStruct((BLK, BLK), F32),
            jax.ShapeDtypeStruct((8, BLK), F32),
        ],
        compiler_params=PARAMS,
        name="spread",
    )(*[pltpu.with_memory_space_constraint(v, pltpu.HBM) for v in (points, lengths, targets)], scale, noise)


ORDER = (0, -1, 1, 4, -3, -2, 2, 3)


def prepare_rows(values, left, left_sq):
    for block, value in enumerate(values):
        value = value * ROOT
        high, low = halves(value)
        at, lanes = block * BLK // TILE, pl.ds(block * BLK % TILE, BLK)
        left[at, pl.ds(0, 128), lanes] = high
        left[at, pl.ds(128, 128), lanes] = low
        left[at, pl.ds(256, 128), lanes] = high
        left[at, pl.ds(384, 128), lanes] = low
        left_sq[at, :, lanes] = -0.5 * jnp.sum(value * value, axis=0, keepdims=True)


def place_of(tile, local):
    return lax.rem(lax.axis_index("z") + (ORDER[tile % 2 * 4 + local] + 8), 8)


def prepare_cols(col_refs, right, right_sq, vecs):
    each = 8 // len(col_refs)
    for block in range(8):
        ref, at = col_refs[block // each], block % each
        value = ref[at, pl.ds(0, BLK), :].T * ROOT
        high, low = halves(value)
        rows = pl.ds(block * BLK, BLK)
        right[rows, pl.ds(0, 128)] = high
        right[rows, pl.ds(128, 128)] = high
        right[rows, pl.ds(256, 128)] = low
        right[rows, pl.ds(384, 128)] = low
        right_sq[rows, :] = -0.5 * jnp.sum(value * value, axis=1, keepdims=True)
        high, low = halves(ref[at, pl.ds(BLK, RHS), :])
        vecs[pl.ds(0, RHS), rows] = high
        vecs[pl.ds(RHS, RHS), rows] = low


def make_values(left, left_sq, right, right_sq, vecs, high, low):
    for step in range(WIDE // SUB):
        rows = pl.ds(step * SUB, SUB)
        power = jnp.dot(right[rows, :], left[...], preferred_element_type=F32)
        high[rows, :], low[rows, :] = halves(jnp.exp2(power + right_sq[rows, :] + left_sq[...]))
    both = jnp.dot(vecs[...], high[...], preferred_element_type=F32)
    rest = jnp.dot(vecs[pl.ds(0, RHS), :], low[...], preferred_element_type=F32)
    product = both[:RHS] + both[RHS:] + rest
    return [product[:, local * BLK : (local + 1) * BLK] for local in range(TILE // BLK)]


def cols_kernel(cols, right, right_sq, vecs):
    prepare_cols((cols,), right, right_sq, vecs)


def own_kernel(count, *refs):
    blocks, (right, right_sq, vecs, out, high, low, left, left_sq) = refs[:count], refs[count:]
    values = []
    for ref in blocks:
        values += [ref[...]] if len(ref.shape) == 2 else [ref[at] for at in range(ref.shape[0])]
    prepare_rows(values, left, left_sq)
    for to in range(len(values) * BLK // TILE):
        made = make_values(left.at[to], left_sq.at[to], right, right_sq, vecs, high.at[to], low.at[to])
        for local, piece in enumerate(made):
            out[to * 4 + local] = piece


def more_kernel(tiles, last, count, *refs):
    cols, refs = refs[:count], refs[count:]
    lefts, befores, (out, high, low, right, right_sq, vecs) = refs[:6], refs[6:-6], refs[-6:]
    prepare_cols(cols, right, right_sq, vecs)
    for to, tile in enumerate(tiles):
        ref, at = WHERE[tile]
        made = make_values(
            lefts[ref].at[at], lefts[3 + ref].at[at], right, right_sq, vecs, high.at[to], low.at[to]
        )
        for local, piece in enumerate(made):
            before = befores[0][tile * 4 + local] if len(befores) == 1 else befores[ref][at * 4 + local]
            out[place_of(tile, local) if last else to * 4 + local] = piece + before


WHERE = ((0, 0), (1, 0), (2, 0), (2, 1))
ALL, MINE, THEIRS = (0, 1, 2, 3), (0, 1), (2, 3)


def made(tiles):
    values = pltpu.VMEM((len(tiles), WIDE, TILE), BF16)
    return [pltpu.VMEM((len(tiles) * TILE // BLK, RHS, BLK), F32), values, values]


def made_cost(tiles):
    width = len(tiles) * TILE
    return cost(2 * width * WIDE * 768, 4 * width * WIDE, width * WIDE)


RIGHT = [pltpu.VMEM((WIDE, 512), BF16), pltpu.VMEM((WIDE, 1), F32), pltpu.VMEM((2 * RHS, WIDE), BF16)]


def own_cols(cols):
    return pl.pallas_call(
        cols_kernel,
        in_specs=[VMEM],
        out_specs=[VMEM] * 3,
        out_shape=RIGHT,
        compiler_params=PARAMS,
        cost_estimate=cost(0, 2 << 20, 0),
        name="own_cols",
    )(cols)


def own_chunk(blocks, cols, tiles):
    return pl.pallas_call(
        functools.partial(own_kernel, len(blocks)),
        in_specs=[VMEM] * (len(blocks) + 3),
        out_specs=[VMEM] * 5,
        out_shape=[*made(tiles), pltpu.VMEM((len(tiles), 512, TILE), BF16), pltpu.VMEM((len(tiles), 1, TILE), F32)],
        compiler_params=PARAMS,
        cost_estimate=made_cost(tiles),
    )(*blocks, *[kept(v) for v in cols])


def more_chunk(tiles, cols, lefts, befores, last=False):
    return pl.pallas_call(
        functools.partial(more_kernel, tiles, last, len(cols)),
        in_specs=[VMEM] * (6 + len(cols) + len(befores)),
        out_specs=[VMEM] * 3,
        out_shape=made(tiles),
        scratch_shapes=RIGHT,
        compiler_params=PARAMS,
        cost_estimate=made_cost(tiles),
    )(*cols, *[kept(v) for v in lefts], *[kept(v) for v in befores])


def total(x):
    return jnp.sum(x, axis=1, keepdims=True)


def between_kernel(aux, arrived, targets, first_ref, wide_ref):
    first = aux[0:1, 0:1] * jnp.sum(arrived[...], axis=0) + aux[1:2, 0:1] * targets[...]
    first_ref[...] = first
    for peer in range(32):
        wide_ref[peer] = first


def between(aux, arrived, targets):
    return pl.pallas_call(
        between_kernel,
        in_specs=[VMEM] * 3,
        out_specs=[VMEM] * 2,
        out_shape=[jax.ShapeDtypeStruct((RHS, BLK), F32), jax.ShapeDtypeStruct((32, RHS, BLK), F32)],
        compiler_params=PARAMS,
        name="between",
    )(aux, arrived, targets)


def second_kernel(tiles, gathered, *refs):
    highs, lows, out, vecs = refs[0:7], refs[7:14], refs[14], refs[15]
    place = lax.axis_index("x")
    for chunk in range(4):
        source = lax.rem(place + (0, 3, 1, 2)[chunk], 4) * 8
        for y in range(8):
            lanes = pl.ds(y * BLK, BLK)
            high, low = halves(gathered[source + y])
            vecs[chunk, pl.ds(0, RHS), lanes] = high
            vecs[chunk, pl.ds(RHS, RHS), lanes] = low
    for tile in tiles:
        product = jnp.zeros((RHS, TILE), F32)
        for chunk in range(4):
            ref, at = ((0, 1, 2, 2)[tile], (0, 0, 0, 1)[tile]) if chunk == 0 else (2 + chunk, tile)
            if chunk == 3:
                ref, at = 5 + tile // 2, tile % 2
            both = jnp.dot(vecs[chunk], highs[ref][at], preferred_element_type=F32)
            rest = jnp.dot(vecs[chunk, pl.ds(0, RHS), :], lows[ref][at], preferred_element_type=F32)
            product = product + both[:RHS] + both[RHS:] + rest
        for local in range(TILE // BLK):
            out[place_of(tile, local)] = product[:, local * BLK : (local + 1) * BLK]


def second(tiles, gathered, highs, lows):
    width = len(tiles) * TILE
    return pl.pallas_call(
        functools.partial(second_kernel, tiles),
        in_specs=[VMEM] * (1 + len(highs) + len(lows)),
        out_specs=VMEM,
        out_shape=pltpu.VMEM((width // BLK, RHS, BLK), F32),
        scratch_shapes=[pltpu.VMEM((4, 2 * RHS, WIDE), BF16)],
        compiler_params=PARAMS,
        cost_estimate=cost(2 * width * 4 * WIDE * 128, 4 * width * 4 * WIDE, 0),
    )(gathered, *[kept(v) for v in highs], *[kept(v) for v in lows])


def total(x):
    return jnp.sum(x, axis=1, keepdims=True)


def settle_kernel(aux, arrived, targets, first_ref, second_ref, dots_ref):
    vectors, first = targets[...], first_ref[...]
    second_image = aux[0:1, 0:1] * jnp.sum(arrived[...], axis=0) + aux[1:2, 0:1] * first
    second_ref[...] = second_image
    dots = (vectors * vectors, vectors * first, first * first, first * second_image)
    lane = lax.broadcasted_iota(jnp.int32, (RHS, BLK), 1)
    wide = jnp.zeros((RHS, BLK), F32)
    for at, dot in enumerate(dots):
        wide = jnp.where(lane == at, total(dot), wide)
    tall = jnp.concatenate([wide, jnp.zeros((BLK - RHS, BLK), F32)], axis=0).T
    row = tall[0:1]
    for at in range(1, 4):
        row = row + pltpu.roll(tall[at : at + 1], at * RHS, 1)
    dots_ref[...] = jnp.broadcast_to(row, (8, BLK))


def settle(aux, arrived, targets, first):
    return pl.pallas_call(
        settle_kernel,
        in_specs=[VMEM] * 4,
        out_specs=[VMEM] * 2,
        out_shape=[jax.ShapeDtypeStruct((RHS, BLK), F32), jax.ShapeDtypeStruct((8, BLK), F32)],
        compiler_params=PARAMS,
        name="settle",
    )(aux, arrived, targets, first)


def finish_kernel(sums, targets, first_ref, second_ref, solution_ref, residual_ref):
    row = jnp.broadcast_to(jnp.sum(sums[...], axis=0), (8, BLK))
    sub = lax.broadcasted_iota(jnp.int32, (8, BLK), 0)
    rows = jnp.zeros((8, BLK), F32)
    for at in range(4):
        rows = jnp.where(sub == at, pltpu.roll(row, (BLK - at * RHS) % BLK, 1), rows)
    tall = jnp.concatenate([rows, jnp.zeros((BLK - 8, BLK), F32)], axis=0).T
    norm, curve, square, cubic = [tall[:RHS, at : at + 1] for at in range(4)]
    vectors, first = targets[...], first_ref[...]
    step = norm / curve
    norm_next = norm - 2.0 * step * curve + step * step * square
    more = 1.0 + norm_next / norm
    new_curve = more * more * curve - 2.0 * step * more * square + step * step * cubic
    new_step = norm_next / new_curve
    solution_ref[...] = step * vectors + new_step * (more * vectors - step * first)
    residual_ref[...] = vectors - step * first - new_step * (more * first - step * second_ref[...])


def finish(sums, targets, first, second_image):
    shape = jax.ShapeDtypeStruct((RHS, BLK), F32)
    return pl.pallas_call(
        finish_kernel,
        in_specs=[VMEM] * 4,
        out_specs=[VMEM] * 2,
        out_shape=[shape, shape],
        compiler_params=PARAMS,
        name="finish",
    )(sums, targets, first, second_image)


def to_each(x, axes):
    peers = lax.axis_size(axes)
    return exchange(jnp.broadcast_to(x[None], (peers, *x.shape)), axes)


def on_device(points, targets, lengthscales, outputscale, noise):
    near, own, aux = spread(points, lengthscales[None], targets, outputscale, noise)
    near = exchange(near, "y")
    behind, ahead = shift(near, "x", 1), shift(near, "x", -1)
    across = [shift(behind[:4], "x", 1), shift(ahead[4:], "x", -1)]
    below, above, far = shift(own, "z", 1), shift(own, "z", -1), shift(own, "z", 4)
    pairs = [shift(jnp.stack([below, own]), "z", 2), shift(jnp.stack([own, above]), "z", -2)]
    prepared = own_cols(near)
    chunks = []
    chunks.append(own_chunk([own, below, above, far], prepared, (0,)))
    same = jnp.concatenate([jnp.stack([own, below, above, far]), *pairs])
    other = shift(same, "c", 1)
    chunks.append(own_chunk(pairs, prepared, (1,)))
    chunks.append(own_chunk([other], prepared, THEIRS))
    pieces, highs, lows, left, left_sq = [list(part) for part in zip(*chunks)]
    lefts = [*left, *left_sq]
    for cols in ([behind], [ahead]):
        piece, high, low = more_chunk(ALL, cols, lefts, pieces)
        pieces = [piece]
        highs.append(high)
        lows.append(low)
    theirs, high_theirs, low_theirs = more_chunk(THEIRS, across, lefts, pieces, True)
    theirs = shift(theirs, "c", 1)
    mine, high_mine, low_mine = more_chunk(MINE, across, lefts, pieces, True)
    highs += [high_mine, high_theirs]
    lows += [low_mine, low_theirs]
    arrived = exchange(mine + theirs, "z")
    first, wide = between(aux, arrived, targets)
    gathered = exchange(wide, ("x", "y"))
    theirs = shift(second(THEIRS, gathered, highs, lows), "c", 1)
    mine = second(MINE, gathered, highs, lows)
    arrived = exchange(mine + theirs, "z")
    second_image, dots = settle(aux, arrived, targets, first)
    sums = jnp.sum(to_each(dots[0:1], "z"), axis=0)
    return tuple(finish(to_each(sums, ("x", "y", "c")), targets, first, second_image))


def solution(mesh):
    finer = Mesh(mesh.devices.reshape(4, 8, 2, mesh.shape["row"]), AXES)
    spec = P(None, AXES)

    return jax.shard_map(
        on_device, mesh=finer, in_specs=(spec, spec, P(), P(), P()), out_specs=(spec, spec), check_vma=False
    )
```

```python
import functools
import math

import jax
import jax.numpy as jnp
from jax import lax
from jax.experimental import pallas as pl
from jax.experimental.pallas import tpu as pltpu
from jax.sharding import Mesh
from jax.sharding import PartitionSpec as P


AXES = ("x", "y", "c", "z")
F32 = jnp.float32
BF16 = jnp.bfloat16
ROOT = math.sqrt(math.log2(math.e))
BLK = 128
RHS = 32
TILE = 512
SUB = 256
WIDE = 1024
VMEM = pl.BlockSpec(memory_space=pltpu.VMEM)
SMEM = pl.BlockSpec(memory_space=pltpu.SMEM)
PARAMS = pltpu.CompilerParams(vmem_limit_bytes=12 << 20)


def shift(value, axis, steps):
    count = lax.axis_size(axis)
    return lax.ppermute(value, axis, [(s, (s + steps) % count) for s in range(count)])


def exchange(x, axes):
    return lax.all_to_all(x, axes, 0, 0, tiled=True)


def halves(x):
    high = x.astype(BF16)
    return high, (x - high.astype(F32)).astype(BF16)


def kept(x):
    return pltpu.with_memory_space_constraint(x, pltpu.VMEM)


def cost(flops=0, moved=0, powers=0):
    return pl.CostEstimate(flops=flops, bytes_accessed=moved, transcendentals=powers)


def spread_kernel(points_in, lengths_in, targets_in, scale, noise, out, own, aux, points, lengths, targets, sems):
    copies = [
        pltpu.make_async_copy(source, to, sems.at[at])
        for at, (source, to) in enumerate(((points_in, points), (lengths_in, lengths), (targets_in, targets)))
    ]
    for copy in copies:
        copy.start()
    for copy in copies:
        copy.wait()
    scaled = points[...] / jnp.broadcast_to(lengths[...], (BLK, BLK)).T
    vectors = targets[...]
    own[...] = scaled
    for peer in range(8):
        out[peer, pl.ds(0, BLK), :] = scaled
        out[peer, pl.ds(BLK, RHS), :] = vectors
    aux[...] = jnp.where(lax.broadcasted_iota(jnp.int32, (8, BLK), 0) == 0, scale[0], noise[0])


def spread(points, lengths, targets, scale, noise):
    return pl.pallas_call(
        spread_kernel,
        in_specs=[pl.BlockSpec(memory_space=pltpu.HBM)] * 3 + [SMEM, SMEM],
        out_specs=[VMEM] * 3,
        scratch_shapes=[
            pltpu.VMEM((BLK, BLK), F32),
            pltpu.VMEM((1, BLK), F32),
            pltpu.VMEM((RHS, BLK), F32),
            pltpu.SemaphoreType.DMA((3,)),
        ],
        out_shape=[
            jax.ShapeDtypeStruct((8, BLK + RHS, BLK), F32),
            jax.ShapeDtypeStruct((BLK, BLK), F32),
            jax.ShapeDtypeStruct((8, BLK), F32),
        ],
        compiler_params=PARAMS,
        name="spread",
    )(*[pltpu.with_memory_space_constraint(v, pltpu.HBM) for v in (points, lengths, targets)], scale, noise)


ORDER = (0, -1, 1, 4, -3, -2, 2, 3)


def prepare_rows(values, left, left_sq):
    for block, value in enumerate(values):
        value = value * ROOT
        high, low = halves(value)
        at, lanes = block * BLK // TILE, pl.ds(block * BLK % TILE, BLK)
        left[at, pl.ds(0, 128), lanes] = high
        left[at, pl.ds(128, 128), lanes] = low
        left[at, pl.ds(256, 128), lanes] = high
        left[at, pl.ds(384, 128), lanes] = low
        left_sq[at, :, lanes] = -0.5 * jnp.sum(value * value, axis=0, keepdims=True)


def place_of(tile, local):
    return lax.rem(lax.axis_index("z") + (ORDER[tile % 2 * 4 + local] + 8), 8)


def prepare_cols(col_refs, right, right_sq, vecs):
    each = 8 // len(col_refs)
    for block in range(8):
        ref, at = col_refs[block // each], block % each
        value = ref[at, pl.ds(0, BLK), :].T * ROOT
        high, low = halves(value)
        rows = pl.ds(block * BLK, BLK)
        right[rows, pl.ds(0, 128)] = high
        right[rows, pl.ds(128, 128)] = high
        right[rows, pl.ds(256, 128)] = low
        right[rows, pl.ds(384, 128)] = low
        right_sq[rows, :] = -0.5 * jnp.sum(value * value, axis=1, keepdims=True)
        high, low = halves(ref[at, pl.ds(BLK, RHS), :])
        vecs[pl.ds(0, RHS), rows] = high
        vecs[pl.ds(RHS, RHS), rows] = low


def make_values(left, left_sq, right, right_sq, vecs, high, low):
    for step in range(WIDE // SUB):
        rows = pl.ds(step * SUB, SUB)
        power = jnp.dot(right[rows, :], left[...], preferred_element_type=F32)
        high[rows, :], low[rows, :] = halves(jnp.exp2(power + right_sq[rows, :] + left_sq[...]))
    both = jnp.dot(vecs[...], high[...], preferred_element_type=F32)
    rest = jnp.dot(vecs[pl.ds(0, RHS), :], low[...], preferred_element_type=F32)
    product = both[:RHS] + both[RHS:] + rest
    return [product[:, local * BLK : (local + 1) * BLK] for local in range(TILE // BLK)]


def cols_kernel(cols, right, right_sq, vecs):
    prepare_cols((cols,), right, right_sq, vecs)


def own_kernel(count, *refs):
    blocks, (right, right_sq, vecs, out, high, low, left, left_sq) = refs[:count], refs[count:]
    values = []
    for ref in blocks:
        values += [ref[...]] if len(ref.shape) == 2 else [ref[at] for at in range(ref.shape[0])]
    prepare_rows(values, left, left_sq)
    for to in range(len(values) * BLK // TILE):
        made = make_values(left.at[to], left_sq.at[to], right, right_sq, vecs, high.at[to], low.at[to])
        for local, piece in enumerate(made):
            out[to * 4 + local] = piece


def more_kernel(tiles, last, count, *refs):
    cols, refs = refs[:count], refs[count:]
    lefts, befores, (out, high, low, right, right_sq, vecs) = refs[:6], refs[6:-6], refs[-6:]
    prepare_cols(cols, right, right_sq, vecs)
    for to, tile in enumerate(tiles):
        ref, at = WHERE[tile]
        made = make_values(
            lefts[ref].at[at], lefts[3 + ref].at[at], right, right_sq, vecs, high.at[to], low.at[to]
        )
        for local, piece in enumerate(made):
            before = befores[0][tile * 4 + local] if len(befores) == 1 else befores[ref][at * 4 + local]
            out[place_of(tile, local) if last else to * 4 + local] = piece + before


WHERE = ((0, 0), (1, 0), (2, 0), (2, 1))
ALL, MINE, THEIRS = (0, 1, 2, 3), (0, 1), (2, 3)


def made(tiles):
    values = pltpu.VMEM((len(tiles), WIDE, TILE), BF16)
    return [pltpu.VMEM((len(tiles) * TILE // BLK, RHS, BLK), F32), values, values]


def made_cost(tiles):
    width = len(tiles) * TILE
    return cost(2 * width * WIDE * 768, 4 * width * WIDE, width * WIDE)


RIGHT = [pltpu.VMEM((WIDE, 512), BF16), pltpu.VMEM((WIDE, 1), F32), pltpu.VMEM((2 * RHS, WIDE), BF16)]


def own_cols(cols):
    return pl.pallas_call(
        cols_kernel,
        in_specs=[VMEM],
        out_specs=[VMEM] * 3,
        out_shape=RIGHT,
        compiler_params=PARAMS,
        cost_estimate=cost(0, 2 << 20, 0),
        name="own_cols",
    )(cols)


def own_chunk(blocks, cols, tiles):
    return pl.pallas_call(
        functools.partial(own_kernel, len(blocks)),
        in_specs=[VMEM] * (len(blocks) + 3),
        out_specs=[VMEM] * 5,
        out_shape=[*made(tiles), pltpu.VMEM((len(tiles), 512, TILE), BF16), pltpu.VMEM((len(tiles), 1, TILE), F32)],
        compiler_params=PARAMS,
        cost_estimate=made_cost(tiles),
    )(*blocks, *[kept(v) for v in cols])


def more_chunk(tiles, cols, lefts, befores, last=False):
    return pl.pallas_call(
        functools.partial(more_kernel, tiles, last, len(cols)),
        in_specs=[VMEM] * (6 + len(cols) + len(befores)),
        out_specs=[VMEM] * 3,
        out_shape=made(tiles),
        scratch_shapes=RIGHT,
        compiler_params=PARAMS,
        cost_estimate=made_cost(tiles),
    )(*cols, *[kept(v) for v in lefts], *[kept(v) for v in befores])


def total(x):
    return jnp.sum(x, axis=1, keepdims=True)


def between_kernel(aux, arrived, targets, first_ref, wide_ref):
    first = aux[0:1, 0:1] * jnp.sum(arrived[...], axis=0) + aux[1:2, 0:1] * targets[...]
    first_ref[...] = first
    for peer in range(32):
        wide_ref[peer] = first


def between(aux, arrived, targets):
    return pl.pallas_call(
        between_kernel,
        in_specs=[VMEM] * 3,
        out_specs=[VMEM] * 2,
        out_shape=[jax.ShapeDtypeStruct((RHS, BLK), F32), jax.ShapeDtypeStruct((32, RHS, BLK), F32)],
        compiler_params=PARAMS,
        name="between",
    )(aux, arrived, targets)


def second_kernel(tiles, gathered, *refs):
    highs, lows, out, vecs = refs[0:7], refs[7:14], refs[14], refs[15]
    place = lax.axis_index("x")
    for chunk in range(4):
        source = lax.rem(place + (0, 3, 1, 2)[chunk], 4) * 8
        for y in range(8):
            lanes = pl.ds(y * BLK, BLK)
            high, low = halves(gathered[source + y])
            vecs[chunk, pl.ds(0, RHS), lanes] = high
            vecs[chunk, pl.ds(RHS, RHS), lanes] = low
    for tile in tiles:
        product = jnp.zeros((RHS, TILE), F32)
        for chunk in range(4):
            ref, at = ((0, 1, 2, 2)[tile], (0, 0, 0, 1)[tile]) if chunk == 0 else (2 + chunk, tile)
            if chunk == 3:
                ref, at = 5 + tile // 2, tile % 2
            both = jnp.dot(vecs[chunk], highs[ref][at], preferred_element_type=F32)
            rest = jnp.dot(vecs[chunk, pl.ds(0, RHS), :], lows[ref][at], preferred_element_type=F32)
            product = product + both[:RHS] + both[RHS:] + rest
        for local in range(TILE // BLK):
            out[place_of(tile, local)] = product[:, local * BLK : (local + 1) * BLK]


def second(tiles, gathered, highs, lows):
    width = len(tiles) * TILE
    return pl.pallas_call(
        functools.partial(second_kernel, tiles),
        in_specs=[VMEM] * (1 + len(highs) + len(lows)),
        out_specs=VMEM,
        out_shape=pltpu.VMEM((width // BLK, RHS, BLK), F32),
        scratch_shapes=[pltpu.VMEM((4, 2 * RHS, WIDE), BF16)],
        compiler_params=PARAMS,
        cost_estimate=cost(2 * width * 4 * WIDE * 128, 4 * width * 4 * WIDE, 0),
    )(gathered, *[kept(v) for v in highs], *[kept(v) for v in lows])


def total(x):
    return jnp.sum(x, axis=1, keepdims=True)


def settle_kernel(aux, arrived, targets, first_ref, second_ref, dots_ref):
    vectors, first = targets[...], first_ref[...]
    second_image = aux[0:1, 0:1] * jnp.sum(arrived[...], axis=0) + aux[1:2, 0:1] * first
    second_ref[...] = second_image
    dots = (vectors * vectors, vectors * first, first * first, first * second_image)
    lane = lax.broadcasted_iota(jnp.int32, (RHS, BLK), 1)
    wide = jnp.zeros((RHS, BLK), F32)
    for at, dot in enumerate(dots):
        wide = jnp.where(lane == at, total(dot), wide)
    tall = jnp.concatenate([wide, jnp.zeros((BLK - RHS, BLK), F32)], axis=0).T
    row = tall[0:1]
    for at in range(1, 4):
        row = row + pltpu.roll(tall[at : at + 1], at * RHS, 1)
    dots_ref[...] = jnp.broadcast_to(row, (8, BLK))


def settle(aux, arrived, targets, first):
    return pl.pallas_call(
        settle_kernel,
        in_specs=[VMEM] * 4,
        out_specs=[VMEM] * 2,
        out_shape=[jax.ShapeDtypeStruct((RHS, BLK), F32), jax.ShapeDtypeStruct((8, BLK), F32)],
        compiler_params=PARAMS,
        name="settle",
    )(aux, arrived, targets, first)


def finish_kernel(sums, targets, first_ref, second_ref, solution_ref, residual_ref):
    row = jnp.broadcast_to(jnp.sum(sums[...], axis=0), (8, BLK))
    sub = lax.broadcasted_iota(jnp.int32, (8, BLK), 0)
    rows = jnp.zeros((8, BLK), F32)
    for at in range(4):
        rows = jnp.where(sub == at, pltpu.roll(row, (BLK - at * RHS) % BLK, 1), rows)
    tall = jnp.concatenate([rows, jnp.zeros((BLK - 8, BLK), F32)], axis=0).T
    norm, curve, square, cubic = [tall[:RHS, at : at + 1] for at in range(4)]
    vectors, first = targets[...], first_ref[...]
    step = norm / curve
    norm_next = norm - 2.0 * step * curve + step * step * square
    more = 1.0 + norm_next / norm
    new_curve = more * more * curve - 2.0 * step * more * square + step * step * cubic
    new_step = norm_next / new_curve
    solution_ref[...] = step * vectors + new_step * (more * vectors - step * first)
    residual_ref[...] = vectors - step * first - new_step * (more * first - step * second_ref[...])


def finish(sums, targets, first, second_image):
    shape = jax.ShapeDtypeStruct((RHS, BLK), F32)
    return pl.pallas_call(
        finish_kernel,
        in_specs=[VMEM] * 4,
        out_specs=[VMEM] * 2,
        out_shape=[shape, shape],
        compiler_params=PARAMS,
        name="finish",
    )(sums, targets, first, second_image)


def received_kernel(behind, ahead, out):
    odd = lax.rem(lax.axis_index("z"), 2) == 1

    @pl.when(odd)
    def _():
        out[...] = ahead[4:]

    @pl.when(jnp.logical_not(odd))
    def _():
        out[...] = behind[4:]


def received(behind, ahead):
    return pl.pallas_call(
        received_kernel,
        in_specs=[VMEM] * 2,
        out_specs=VMEM,
        out_shape=jax.ShapeDtypeStruct((4, *behind.shape[1:]), F32),
        compiler_params=PARAMS,
        cost_estimate=cost(0, 1 << 20, 0),
        name="received",
    )(behind, ahead)


def to_each(x, axes):
    peers = lax.axis_size(axes)
    return exchange(jnp.broadcast_to(x[None], (peers, *x.shape)), axes)


def on_device(points, targets, lengthscales, outputscale, noise):
    near, own, aux = spread(points, lengthscales[None], targets, outputscale, noise)
    near = exchange(near, "y")
    behind, ahead = shift(near, "x", 1), shift(near, "x", -1)
    across = [shift(near[:4], "x", 2)]
    onward = received(behind, ahead)
    hops = [(x * 8 + z, (x + (3 if z % 2 else 1)) % 4 * 8 + z) for x in range(4) for z in range(8)]
    across.append(lax.ppermute(onward, ("x", "z"), hops))
    below, above, far = shift(own, "z", 1), shift(own, "z", -1), shift(own, "z", 4)
    pairs = [shift(jnp.stack([below, own]), "z", 2), shift(jnp.stack([own, above]), "z", -2)]
    prepared = own_cols(near)
    chunks = []
    chunks.append(own_chunk([own, below, above, far], prepared, (0,)))
    same = jnp.concatenate([jnp.stack([own, below, above, far]), *pairs])
    other = shift(same, "c", 1)
    chunks.append(own_chunk(pairs, prepared, (1,)))
    chunks.append(own_chunk([other], prepared, THEIRS))
    pieces, highs, lows, left, left_sq = [list(part) for part in zip(*chunks)]
    lefts = [*left, *left_sq]
    for cols in ([behind], [ahead]):
        piece, high, low = more_chunk(ALL, cols, lefts, pieces)
        pieces = [piece]
        highs.append(high)
        lows.append(low)
    theirs, high_theirs, low_theirs = more_chunk(THEIRS, across, lefts, pieces, True)
    theirs = shift(theirs, "c", 1)
    mine, high_mine, low_mine = more_chunk(MINE, across, lefts, pieces, True)
    highs += [high_mine, high_theirs]
    lows += [low_mine, low_theirs]
    arrived = exchange(mine + theirs, "z")
    first, wide = between(aux, arrived, targets)
    gathered = exchange(wide, ("x", "y"))
    theirs = shift(second(THEIRS, gathered, highs, lows), "c", 1)
    mine = second(MINE, gathered, highs, lows)
    arrived = exchange(mine + theirs, "z")
    second_image, dots = settle(aux, arrived, targets, first)
    sums = jnp.sum(to_each(dots[0:1], ("y", "c")), axis=0)
    return tuple(finish(to_each(sums, ("x", "z")), targets, first, second_image))


def solution(mesh):
    finer = Mesh(mesh.devices.reshape(4, 8, 2, mesh.shape["row"]), AXES)
    spec = P(None, AXES)

    return jax.shard_map(
        on_device, mesh=finer, in_specs=(spec, spec, P(), P(), P()), out_specs=(spec, spec), check_vma=False
    )
```

```python
import functools
import math

import jax
import jax.numpy as jnp
from jax import lax
from jax.experimental import pallas as pl
from jax.experimental.pallas import tpu as pltpu
from jax.sharding import Mesh
from jax.sharding import PartitionSpec as P


AXES = ("x", "y", "c", "z")
F32 = jnp.float32
BF16 = jnp.bfloat16
ROOT = math.sqrt(math.log2(math.e))
BLK = 128
RHS = 32
TILE = 512
SUB = 256
WIDE = 1024
VMEM = pl.BlockSpec(memory_space=pltpu.VMEM)
SMEM = pl.BlockSpec(memory_space=pltpu.SMEM)
PARAMS = pltpu.CompilerParams(vmem_limit_bytes=12 << 20)


def shift(value, axis, steps):
    count = lax.axis_size(axis)
    return lax.ppermute(value, axis, [(s, (s + steps) % count) for s in range(count)])


def exchange(x, axes):
    return lax.all_to_all(x, axes, 0, 0, tiled=True)


def halves(x):
    high = x.astype(BF16)
    return high, (x - high.astype(F32)).astype(BF16)


def kept(x):
    return pltpu.with_memory_space_constraint(x, pltpu.VMEM)


def cost(flops=0, moved=0, powers=0):
    return pl.CostEstimate(flops=flops, bytes_accessed=moved, transcendentals=powers)


def spread_kernel(points_in, lengths_in, targets_in, scale, noise, out, own, aux, points, lengths, targets, sems):
    copies = [
        pltpu.make_async_copy(source, to, sems.at[at])
        for at, (source, to) in enumerate(((points_in, points), (lengths_in, lengths), (targets_in, targets)))
    ]
    for copy in copies:
        copy.start()
    for copy in copies:
        copy.wait()
    scaled = points[...] / jnp.broadcast_to(lengths[...], (BLK, BLK)).T
    vectors = targets[...]
    own[...] = scaled
    for peer in range(8):
        out[peer, pl.ds(0, BLK), :] = scaled
        out[peer, pl.ds(BLK, RHS), :] = vectors
    aux[...] = jnp.where(lax.broadcasted_iota(jnp.int32, (8, BLK), 0) == 0, scale[0], noise[0])


def spread(points, lengths, targets, scale, noise):
    return pl.pallas_call(
        spread_kernel,
        in_specs=[pl.BlockSpec(memory_space=pltpu.HBM)] * 3 + [SMEM, SMEM],
        out_specs=[VMEM] * 3,
        scratch_shapes=[
            pltpu.VMEM((BLK, BLK), F32),
            pltpu.VMEM((1, BLK), F32),
            pltpu.VMEM((RHS, BLK), F32),
            pltpu.SemaphoreType.DMA((3,)),
        ],
        out_shape=[
            jax.ShapeDtypeStruct((8, BLK + RHS, BLK), F32),
            jax.ShapeDtypeStruct((BLK, BLK), F32),
            jax.ShapeDtypeStruct((8, BLK), F32),
        ],
        compiler_params=PARAMS,
        name="spread",
    )(*[pltpu.with_memory_space_constraint(v, pltpu.HBM) for v in (points, lengths, targets)], scale, noise)


ORDER = (0, -1, 1, 4, -3, -2, 2, 3)


def prepare_rows(values, left, left_sq):
    for block, value in enumerate(values):
        value = value * ROOT
        high, low = halves(value)
        at, lanes = block * BLK // TILE, pl.ds(block * BLK % TILE, BLK)
        left[at, pl.ds(0, 128), lanes] = high
        left[at, pl.ds(128, 128), lanes] = low
        left[at, pl.ds(256, 128), lanes] = high
        left[at, pl.ds(384, 128), lanes] = low
        left_sq[at, :, lanes] = -0.5 * jnp.sum(value * value, axis=0, keepdims=True)


def place_of(tile, local):
    return lax.rem(lax.axis_index("z") + (ORDER[tile % 2 * 4 + local] + 8), 8)


def prepare_cols(col_refs, right, right_sq, vecs):
    each = 8 // len(col_refs)
    for block in range(8):
        ref, at = col_refs[block // each], block % each
        value = ref[at, pl.ds(0, BLK), :].T * ROOT
        high, low = halves(value)
        rows = pl.ds(block * BLK, BLK)
        right[rows, pl.ds(0, 128)] = high
        right[rows, pl.ds(128, 128)] = high
        right[rows, pl.ds(256, 128)] = low
        right[rows, pl.ds(384, 128)] = low
        right_sq[rows, :] = -0.5 * jnp.sum(value * value, axis=1, keepdims=True)
        high, low = halves(ref[at, pl.ds(BLK, RHS), :])
        vecs[pl.ds(0, RHS), rows] = high
        vecs[pl.ds(RHS, RHS), rows] = low


def make_values(left, left_sq, right, right_sq, vecs, high, low):
    for step in range(WIDE // SUB):
        rows = pl.ds(step * SUB, SUB)
        power = jnp.dot(right[rows, :], left[...], preferred_element_type=F32)
        high[rows, :], low[rows, :] = halves(jnp.exp2(power + right_sq[rows, :] + left_sq[...]))
    both = jnp.dot(vecs[...], high[...], preferred_element_type=F32)
    rest = jnp.dot(vecs[pl.ds(0, RHS), :], low[...], preferred_element_type=F32)
    product = both[:RHS] + both[RHS:] + rest
    return [product[:, local * BLK : (local + 1) * BLK] for local in range(TILE // BLK)]


def cols_kernel(cols, right, right_sq, vecs):
    prepare_cols((cols,), right, right_sq, vecs)


def own_kernel(count, *refs):
    blocks, (right, right_sq, vecs, out, high, low, left, left_sq) = refs[:count], refs[count:]
    values = []
    for ref in blocks:
        values += [ref[...]] if len(ref.shape) == 2 else [ref[at] for at in range(ref.shape[0])]
    prepare_rows(values, left, left_sq)
    for to in range(len(values) * BLK // TILE):
        made = make_values(left.at[to], left_sq.at[to], right, right_sq, vecs, high.at[to], low.at[to])
        for local, piece in enumerate(made):
            out[to * 4 + local] = piece


def more_kernel(tiles, last, cols, *refs):
    lefts, befores, (out, high, low, right, right_sq, vecs) = refs[:6], refs[6:-6], refs[-6:]
    prepare_cols((cols,), right, right_sq, vecs)
    for to, tile in enumerate(tiles):
        ref, at = WHERE[tile]
        made = make_values(
            lefts[ref].at[at], lefts[3 + ref].at[at], right, right_sq, vecs, high.at[to], low.at[to]
        )
        for local, piece in enumerate(made):
            before = befores[0][tile * 4 + local] if len(befores) == 1 else befores[ref][at * 4 + local]
            out[place_of(tile, local) if last else to * 4 + local] = piece + before


WHERE = ((0, 0), (1, 0), (2, 0), (2, 1))
ALL, MINE, THEIRS = (0, 1, 2, 3), (0, 1), (2, 3)


def made(tiles):
    values = pltpu.VMEM((len(tiles), WIDE, TILE), BF16)
    return [pltpu.VMEM((len(tiles) * TILE // BLK, RHS, BLK), F32), values, values]


def made_cost(tiles):
    width = len(tiles) * TILE
    return cost(2 * width * WIDE * 768, 4 * width * WIDE, width * WIDE)


RIGHT = [pltpu.VMEM((WIDE, 512), BF16), pltpu.VMEM((WIDE, 1), F32), pltpu.VMEM((2 * RHS, WIDE), BF16)]


def own_cols(cols):
    return pl.pallas_call(
        cols_kernel,
        in_specs=[VMEM],
        out_specs=[VMEM] * 3,
        out_shape=RIGHT,
        compiler_params=PARAMS,
        cost_estimate=cost(0, 2 << 20, 0),
        name="own_cols",
    )(cols)


def own_chunk(blocks, cols, tiles):
    return pl.pallas_call(
        functools.partial(own_kernel, len(blocks)),
        in_specs=[VMEM] * (len(blocks) + 3),
        out_specs=[VMEM] * 5,
        out_shape=[*made(tiles), pltpu.VMEM((len(tiles), 512, TILE), BF16), pltpu.VMEM((len(tiles), 1, TILE), F32)],
        compiler_params=PARAMS,
        cost_estimate=made_cost(tiles),
    )(*blocks, *[kept(v) for v in cols])


def more_chunk(tiles, cols, lefts, befores, last=False):
    return pl.pallas_call(
        functools.partial(more_kernel, tiles, last),
        in_specs=[VMEM] * (7 + len(befores)),
        out_specs=[VMEM] * 3,
        out_shape=made(tiles),
        scratch_shapes=RIGHT,
        compiler_params=PARAMS,
        cost_estimate=made_cost(tiles),
    )(cols, *[kept(v) for v in lefts], *[kept(v) for v in befores])


def total(x):
    return jnp.sum(x, axis=1, keepdims=True)


def between_kernel(aux, arrived, targets, first_ref, wide_ref):
    first = aux[0:1, 0:1] * jnp.sum(arrived[...], axis=0) + aux[1:2, 0:1] * targets[...]
    first_ref[...] = first
    for peer in range(32):
        wide_ref[peer] = first


def between(aux, arrived, targets):
    return pl.pallas_call(
        between_kernel,
        in_specs=[VMEM] * 3,
        out_specs=[VMEM] * 2,
        out_shape=[jax.ShapeDtypeStruct((RHS, BLK), F32), jax.ShapeDtypeStruct((32, RHS, BLK), F32)],
        compiler_params=PARAMS,
        name="between",
    )(aux, arrived, targets)


def split_vectors(gathered, vecs):
    place = lax.axis_index("x")
    for chunk in range(4):
        source = lax.rem(place + (0, 3, 1, 2)[chunk], 4) * 8
        for y in range(8):
            lanes = pl.ds(y * BLK, BLK)
            high, low = halves(gathered[source + y])
            vecs[chunk, pl.ds(0, RHS), lanes] = high
            vecs[chunk, pl.ds(RHS, RHS), lanes] = low


def second_kernel(tiles, fresh, source, *refs):
    highs, lows, out = refs[0:7], refs[7:14], refs[14]
    vecs = refs[15] if fresh else source
    if fresh:
        split_vectors(source, vecs)
    for tile in tiles:
        product = jnp.zeros((RHS, TILE), F32)
        for chunk in range(4):
            ref, at = ((0, 1, 2, 2)[tile], (0, 0, 0, 1)[tile]) if chunk == 0 else (2 + chunk, tile)
            if chunk == 3:
                ref, at = 5 + tile // 2, tile % 2
            both = jnp.dot(vecs[chunk], highs[ref][at], preferred_element_type=F32)
            rest = jnp.dot(vecs[chunk, pl.ds(0, RHS), :], lows[ref][at], preferred_element_type=F32)
            product = product + both[:RHS] + both[RHS:] + rest
        for local in range(TILE // BLK):
            out[place_of(tile, local)] = product[:, local * BLK : (local + 1) * BLK]


def second(tiles, fresh, source, highs, lows):
    width = len(tiles) * TILE
    out = [pltpu.VMEM((width // BLK, RHS, BLK), F32), pltpu.VMEM((4, 2 * RHS, WIDE), BF16)]
    return pl.pallas_call(
        functools.partial(second_kernel, tiles, fresh),
        in_specs=[VMEM] * (1 + len(highs) + len(lows)),
        out_specs=[VMEM] * (1 + fresh),
        out_shape=out[: 1 + fresh],
        compiler_params=PARAMS,
        cost_estimate=cost(2 * width * 4 * WIDE * 128, 4 * width * 4 * WIDE, 0),
    )(source if fresh else kept(source), *[kept(v) for v in highs], *[kept(v) for v in lows])


def total(x):
    return jnp.sum(x, axis=1, keepdims=True)


def settle_kernel(aux, arrived, targets, first_ref, second_ref, dots_ref):
    vectors, first = targets[...], first_ref[...]
    second_image = aux[0:1, 0:1] * jnp.sum(arrived[...], axis=0) + aux[1:2, 0:1] * first
    second_ref[...] = second_image
    dots = (vectors * vectors, vectors * first, first * first, first * second_image)
    lane = lax.broadcasted_iota(jnp.int32, (RHS, BLK), 1)
    wide = jnp.zeros((RHS, BLK), F32)
    for at, dot in enumerate(dots):
        wide = jnp.where(lane == at, total(dot), wide)
    tall = jnp.concatenate([wide, jnp.zeros((BLK - RHS, BLK), F32)], axis=0).T
    row = tall[0:1]
    for at in range(1, 4):
        row = row + pltpu.roll(tall[at : at + 1], at * RHS, 1)
    dots_ref[...] = jnp.broadcast_to(row, (8, BLK))


def settle(aux, arrived, targets, first):
    return pl.pallas_call(
        settle_kernel,
        in_specs=[VMEM] * 4,
        out_specs=[VMEM] * 2,
        out_shape=[jax.ShapeDtypeStruct((RHS, BLK), F32), jax.ShapeDtypeStruct((8, BLK), F32)],
        compiler_params=PARAMS,
        name="settle",
    )(aux, arrived, targets, first)


def finish_kernel(sums, targets, first_ref, second_ref, solution_ref, residual_ref):
    row = jnp.broadcast_to(jnp.sum(sums[...], axis=0), (8, BLK))
    sub = lax.broadcasted_iota(jnp.int32, (8, BLK), 0)
    rows = jnp.zeros((8, BLK), F32)
    for at in range(4):
        rows = jnp.where(sub == at, pltpu.roll(row, (BLK - at * RHS) % BLK, 1), rows)
    tall = jnp.concatenate([rows, jnp.zeros((BLK - 8, BLK), F32)], axis=0).T
    norm, curve, square, cubic = [tall[:RHS, at : at + 1] for at in range(4)]
    vectors, first = targets[...], first_ref[...]
    step = norm / curve
    norm_next = norm - 2.0 * step * curve + step * step * square
    more = 1.0 + norm_next / norm
    new_curve = more * more * curve - 2.0 * step * more * square + step * step * cubic
    new_step = norm_next / new_curve
    solution_ref[...] = step * vectors + new_step * (more * vectors - step * first)
    residual_ref[...] = vectors - step * first - new_step * (more * first - step * second_ref[...])


def finish(sums, targets, first, second_image):
    shape = jax.ShapeDtypeStruct((RHS, BLK), F32)
    return pl.pallas_call(
        finish_kernel,
        in_specs=[VMEM] * 4,
        out_specs=[VMEM] * 2,
        out_shape=[shape, shape],
        compiler_params=PARAMS,
        name="finish",
    )(sums, targets, first, second_image)


def to_each(x, axes):
    peers = lax.axis_size(axes)
    return exchange(jnp.broadcast_to(x[None], (peers, *x.shape)), axes)


def on_device(points, targets, lengthscales, outputscale, noise):
    near, own, aux = spread(points, lengthscales[None], targets, outputscale, noise)
    near = exchange(near, "y")
    behind, ahead = shift(near, "x", 1), shift(near, "x", -1)
    across = shift(near, "x", 2)
    below, above, far = shift(own, "z", 1), shift(own, "z", -1), shift(own, "z", 4)
    pairs = [shift(jnp.stack([below, own]), "z", 2), shift(jnp.stack([own, above]), "z", -2)]
    prepared = own_cols(near)
    chunks = []
    chunks.append(own_chunk([own, below, above, far], prepared, (0,)))
    same = jnp.concatenate([jnp.stack([own, below, above, far]), *pairs])
    other = shift(same, "c", 1)
    chunks.append(own_chunk(pairs, prepared, (1,)))
    chunks.append(own_chunk([other], prepared, THEIRS))
    pieces, highs, lows, left, left_sq = [list(part) for part in zip(*chunks)]
    lefts = [*left, *left_sq]
    for cols in (behind, ahead):
        piece, high, low = more_chunk(ALL, cols, lefts, pieces)
        pieces = [piece]
        highs.append(high)
        lows.append(low)
    theirs, high_theirs, low_theirs = more_chunk(THEIRS, across, lefts, pieces, True)
    theirs = shift(theirs, "c", 1)
    mine, high_mine, low_mine = more_chunk(MINE, across, lefts, pieces, True)
    highs += [high_mine, high_theirs]
    lows += [low_mine, low_theirs]
    arrived = exchange(mine + theirs, "z")
    first, wide = between(aux, arrived, targets)
    gathered = exchange(wide, ("x", "y"))
    theirs, vecs = second(THEIRS, True, gathered, highs, lows)
    theirs = shift(theirs, "c", 1)
    (mine,) = second(MINE, False, vecs, highs, lows)
    arrived = exchange(mine + theirs, "z")
    second_image, dots = settle(aux, arrived, targets, first)
    sums = jnp.sum(to_each(dots[0:1], ("x", "c")), axis=0)
    return tuple(finish(to_each(sums, ("y", "z")), targets, first, second_image))


def solution(mesh):
    finer = Mesh(mesh.devices.reshape(4, 8, 2, mesh.shape["row"]), AXES)
    spec = P(None, AXES)

    return jax.shard_map(
        on_device, mesh=finer, in_specs=(spec, spec, P(), P(), P()), out_specs=(spec, spec), check_vma=False
    )
```

```python
import functools
import math

import jax
import jax.numpy as jnp
from jax import lax
from jax.experimental import pallas as pl
from jax.experimental.pallas import tpu as pltpu
from jax.sharding import Mesh
from jax.sharding import PartitionSpec as P


AXES = ("x", "y", "c", "z")
F32 = jnp.float32
BF16 = jnp.bfloat16
ROOT = math.sqrt(math.log2(math.e))
BLK = 128
RHS = 32
TILE = 512
SUB = 256
WIDE = 1024
VMEM = pl.BlockSpec(memory_space=pltpu.VMEM)
SMEM = pl.BlockSpec(memory_space=pltpu.SMEM)
PARAMS = pltpu.CompilerParams(vmem_limit_bytes=12 << 20)


def shift(value, axis, steps):
    count = lax.axis_size(axis)
    return lax.ppermute(value, axis, [(s, (s + steps) % count) for s in range(count)])


def exchange(x, axes):
    return lax.all_to_all(x, axes, 0, 0, tiled=True)


def halves(x):
    high = x.astype(BF16)
    return high, (x - high.astype(F32)).astype(BF16)


def kept(x):
    return pltpu.with_memory_space_constraint(x, pltpu.VMEM)


def cost(flops=0, moved=0, powers=0):
    return pl.CostEstimate(flops=flops, bytes_accessed=moved, transcendentals=powers)


def spread_kernel(points_in, lengths_in, targets_in, scale, noise, out, own, aux, points, lengths, targets, sems):
    copies = [
        pltpu.make_async_copy(source, to, sems.at[at])
        for at, (source, to) in enumerate(((points_in, points), (lengths_in, lengths), (targets_in, targets)))
    ]
    for copy in copies:
        copy.start()
    for copy in copies:
        copy.wait()
    scaled = points[...] / jnp.broadcast_to(lengths[...], (BLK, BLK)).T
    vectors = targets[...]
    own[...] = scaled
    for peer in range(8):
        out[peer, pl.ds(0, BLK), :] = scaled
        out[peer, pl.ds(BLK, RHS), :] = vectors
    aux[...] = jnp.where(lax.broadcasted_iota(jnp.int32, (8, BLK), 0) == 0, scale[0], noise[0])


def spread(points, lengths, targets, scale, noise):
    return pl.pallas_call(
        spread_kernel,
        in_specs=[pl.BlockSpec(memory_space=pltpu.HBM)] * 3 + [SMEM, SMEM],
        out_specs=[VMEM] * 3,
        scratch_shapes=[
            pltpu.VMEM((BLK, BLK), F32),
            pltpu.VMEM((1, BLK), F32),
            pltpu.VMEM((RHS, BLK), F32),
            pltpu.SemaphoreType.DMA((3,)),
        ],
        out_shape=[
            jax.ShapeDtypeStruct((8, BLK + RHS, BLK), F32),
            jax.ShapeDtypeStruct((BLK, BLK), F32),
            jax.ShapeDtypeStruct((8, BLK), F32),
        ],
        compiler_params=PARAMS,
        name="spread",
    )(*[pltpu.with_memory_space_constraint(v, pltpu.HBM) for v in (points, lengths, targets)], scale, noise)


ORDER = (0, -1, 1, 4, -3, -2, 2, 3)


def prepare_rows(values, left, left_sq):
    for block, value in enumerate(values):
        value = value * ROOT
        high, low = halves(value)
        at, lanes = block * BLK // TILE, pl.ds(block * BLK % TILE, BLK)
        left[at, pl.ds(0, 128), lanes] = high
        left[at, pl.ds(128, 128), lanes] = low
        left[at, pl.ds(256, 128), lanes] = high
        left[at, pl.ds(384, 128), lanes] = low
        left_sq[at, :, lanes] = -0.5 * jnp.sum(value * value, axis=0, keepdims=True)


def place_of(tile, local):
    return lax.rem(lax.axis_index("z") + (ORDER[tile % 2 * 4 + local] + 8), 8)


def prepare_cols(col_refs, right, right_sq, vecs):
    each = 8 // len(col_refs)
    for block in range(8):
        ref, at = col_refs[block // each], block % each
        value = ref[at, pl.ds(0, BLK), :].T * ROOT
        high, low = halves(value)
        rows = pl.ds(block * BLK, BLK)
        right[rows, pl.ds(0, 128)] = high
        right[rows, pl.ds(128, 128)] = high
        right[rows, pl.ds(256, 128)] = low
        right[rows, pl.ds(384, 128)] = low
        right_sq[rows, :] = -0.5 * jnp.sum(value * value, axis=1, keepdims=True)
        high, low = halves(ref[at, pl.ds(BLK, RHS), :])
        vecs[pl.ds(0, RHS), rows] = high
        vecs[pl.ds(RHS, RHS), rows] = low


def make_values(left, left_sq, right, right_sq, vecs, high, low):
    for step in range(WIDE // SUB):
        rows = pl.ds(step * SUB, SUB)
        power = jnp.dot(right[rows, :], left[...], preferred_element_type=F32)
        high[rows, :], low[rows, :] = halves(jnp.exp2(power + right_sq[rows, :] + left_sq[...]))
    both = jnp.dot(vecs[...], high[...], preferred_element_type=F32)
    rest = jnp.dot(vecs[pl.ds(0, RHS), :], low[...], preferred_element_type=F32)
    product = both[:RHS] + both[RHS:] + rest
    return [product[:, local * BLK : (local + 1) * BLK] for local in range(TILE // BLK)]


def cols_kernel(cols, right, right_sq, vecs):
    prepare_cols((cols,), right, right_sq, vecs)


def own_kernel(count, *refs):
    blocks, (right, right_sq, vecs, out, high, low, left, left_sq) = refs[:count], refs[count:]
    values = []
    for ref in blocks:
        values += [ref[...]] if len(ref.shape) == 2 else [ref[at] for at in range(ref.shape[0])]
    prepare_rows(values, left, left_sq)
    for to in range(len(values) * BLK // TILE):
        made = make_values(left.at[to], left_sq.at[to], right, right_sq, vecs, high.at[to], low.at[to])
        for local, piece in enumerate(made):
            out[to * 4 + local] = piece


def more_kernel(tiles, last, cols, *refs):
    lefts, befores, (out, high, low, right, right_sq, vecs) = refs[:6], refs[6:-6], refs[-6:]
    prepare_cols((cols,), right, right_sq, vecs)
    for to, tile in enumerate(tiles):
        ref, at = WHERE[tile]
        made = make_values(
            lefts[ref].at[at], lefts[3 + ref].at[at], right, right_sq, vecs, high.at[to], low.at[to]
        )
        for local, piece in enumerate(made):
            before = befores[0][tile * 4 + local] if len(befores) == 1 else befores[ref][at * 4 + local]
            out[place_of(tile, local) if last else to * 4 + local] = piece + before


WHERE = ((0, 0), (1, 0), (2, 0), (2, 1))
ALL, MINE, THEIRS = (0, 1, 2, 3), (0, 1), (2, 3)


def made(tiles):
    values = pltpu.VMEM((len(tiles), WIDE, TILE), BF16)
    return [pltpu.VMEM((len(tiles) * TILE // BLK, RHS, BLK), F32), values, values]


def made_cost(tiles):
    width = len(tiles) * TILE
    return cost(2 * width * WIDE * 768, 4 * width * WIDE, width * WIDE)


RIGHT = [pltpu.VMEM((WIDE, 512), BF16), pltpu.VMEM((WIDE, 1), F32), pltpu.VMEM((2 * RHS, WIDE), BF16)]


def own_cols(cols):
    return pl.pallas_call(
        cols_kernel,
        in_specs=[VMEM],
        out_specs=[VMEM] * 3,
        out_shape=RIGHT,
        compiler_params=PARAMS,
        cost_estimate=cost(0, 2 << 20, 0),
        name="own_cols",
    )(cols)


def own_chunk(blocks, cols, tiles):
    return pl.pallas_call(
        functools.partial(own_kernel, len(blocks)),
        in_specs=[VMEM] * (len(blocks) + 3),
        out_specs=[VMEM] * 5,
        out_shape=[*made(tiles), pltpu.VMEM((len(tiles), 512, TILE), BF16), pltpu.VMEM((len(tiles), 1, TILE), F32)],
        compiler_params=PARAMS,
        cost_estimate=made_cost(tiles),
    )(*blocks, *[kept(v) for v in cols])


def more_chunk(tiles, cols, lefts, befores, last=False):
    return pl.pallas_call(
        functools.partial(more_kernel, tiles, last),
        in_specs=[VMEM] * (7 + len(befores)),
        out_specs=[VMEM] * 3,
        out_shape=made(tiles),
        scratch_shapes=RIGHT,
        compiler_params=PARAMS,
        cost_estimate=made_cost(tiles),
    )(cols, *[kept(v) for v in lefts], *[kept(v) for v in befores])


def total(x):
    return jnp.sum(x, axis=1, keepdims=True)


def between_kernel(aux, arrived, targets, first_ref, wide_ref):
    first = aux[0:1, 0:1] * jnp.sum(arrived[...], axis=0) + aux[1:2, 0:1] * targets[...]
    first_ref[...] = first
    for peer in range(32):
        wide_ref[peer] = first


def between(aux, arrived, targets):
    return pl.pallas_call(
        between_kernel,
        in_specs=[VMEM] * 3,
        out_specs=[VMEM] * 2,
        out_shape=[jax.ShapeDtypeStruct((RHS, BLK), F32), jax.ShapeDtypeStruct((32, RHS, BLK), F32)],
        compiler_params=PARAMS,
        name="between",
    )(aux, arrived, targets)


def second_kernel(tiles, gathered, *refs):
    highs, lows, out, vecs = refs[0:7], refs[7:14], refs[14], refs[15]
    place = lax.axis_index("x")
    for chunk in range(4):
        source = lax.rem(place + (0, 3, 1, 2)[chunk], 4) * 8
        for y in range(8):
            lanes = pl.ds(y * BLK, BLK)
            high, low = halves(gathered[source + y])
            vecs[chunk, pl.ds(0, RHS), lanes] = high
            vecs[chunk, pl.ds(RHS, RHS), lanes] = low
    for tile in tiles:
        product = jnp.zeros((RHS, TILE), F32)
        for chunk in range(4):
            ref, at = ((0, 1, 2, 2)[tile], (0, 0, 0, 1)[tile]) if chunk == 0 else (2 + chunk, tile)
            if chunk == 3:
                ref, at = 5 + tile // 2, tile % 2
            both = jnp.dot(vecs[chunk], highs[ref][at], preferred_element_type=F32)
            rest = jnp.dot(vecs[chunk, pl.ds(0, RHS), :], lows[ref][at], preferred_element_type=F32)
            product = product + both[:RHS] + both[RHS:] + rest
        for local in range(TILE // BLK):
            out[place_of(tile, local)] = product[:, local * BLK : (local + 1) * BLK]


def second(tiles, gathered, highs, lows):
    width = len(tiles) * TILE
    return pl.pallas_call(
        functools.partial(second_kernel, tiles),
        in_specs=[VMEM] * (1 + len(highs) + len(lows)),
        out_specs=VMEM,
        out_shape=pltpu.VMEM((width // BLK, RHS, BLK), F32),
        scratch_shapes=[pltpu.VMEM((4, 2 * RHS, WIDE), BF16)],
        compiler_params=PARAMS,
        cost_estimate=cost(2 * width * 4 * WIDE * 128, 4 * width * 4 * WIDE, 0),
    )(gathered, *[kept(v) for v in highs], *[kept(v) for v in lows])


def total(x):
    return jnp.sum(x, axis=1, keepdims=True)


def settle_kernel(aux, arrived, targets, first_ref, second_ref, dots_ref):
    vectors, first = targets[...], first_ref[...]
    second_image = aux[0:1, 0:1] * jnp.sum(arrived[...], axis=0) + aux[1:2, 0:1] * first
    second_ref[...] = second_image
    dots = (vectors * vectors, vectors * first, first * first, first * second_image)
    lane = lax.broadcasted_iota(jnp.int32, (RHS, BLK), 1)
    wide = jnp.zeros((RHS, BLK), F32)
    for at, dot in enumerate(dots):
        wide = jnp.where(lane == at, total(dot), wide)
    tall = jnp.concatenate([wide, jnp.zeros((BLK - RHS, BLK), F32)], axis=0).T
    row = tall[0:1]
    for at in range(1, 4):
        row = row + pltpu.roll(tall[at : at + 1], at * RHS, 1)
    dots_ref[...] = jnp.broadcast_to(row, (8, BLK))


def settle(aux, arrived, targets, first):
    return pl.pallas_call(
        settle_kernel,
        in_specs=[VMEM] * 4,
        out_specs=[VMEM] * 2,
        out_shape=[jax.ShapeDtypeStruct((RHS, BLK), F32), jax.ShapeDtypeStruct((8, BLK), F32)],
        compiler_params=PARAMS,
        name="settle",
    )(aux, arrived, targets, first)


def finish_kernel(sums, targets, first_ref, second_ref, solution_ref, residual_ref):
    row = jnp.broadcast_to(jnp.sum(sums[...], axis=0), (8, BLK))
    sub = lax.broadcasted_iota(jnp.int32, (8, BLK), 0)
    rows = jnp.zeros((8, BLK), F32)
    for at in range(4):
        rows = jnp.where(sub == at, pltpu.roll(row, (BLK - at * RHS) % BLK, 1), rows)
    tall = jnp.concatenate([rows, jnp.zeros((BLK - 8, BLK), F32)], axis=0).T
    norm, curve, square, cubic = [tall[:RHS, at : at + 1] for at in range(4)]
    vectors, first = targets[...], first_ref[...]
    step = norm / curve
    norm_next = norm - 2.0 * step * curve + step * step * square
    more = 1.0 + norm_next / norm
    new_curve = more * more * curve - 2.0 * step * more * square + step * step * cubic
    new_step = norm_next / new_curve
    solution_ref[...] = step * vectors + new_step * (more * vectors - step * first)
    residual_ref[...] = vectors - step * first - new_step * (more * first - step * second_ref[...])


def finish(sums, targets, first, second_image):
    shape = jax.ShapeDtypeStruct((RHS, BLK), F32)
    return pl.pallas_call(
        finish_kernel,
        in_specs=[VMEM] * 4,
        out_specs=[VMEM] * 2,
        out_shape=[shape, shape],
        compiler_params=PARAMS,
        name="finish",
    )(sums, targets, first, second_image)


def to_each(x, axes):
    peers = lax.axis_size(axes)
    return exchange(jnp.broadcast_to(x[None], (peers, *x.shape)), axes)


def on_device(points, targets, lengthscales, outputscale, noise):
    near, own, aux = spread(points, lengthscales[None], targets, outputscale, noise)
    near = exchange(near, "y")
    ahead = shift(near, "x", -1)
    behind = shift(near, "x", 1)
    across = shift(near, "x", 2)
    below, above, far = shift(own, "z", 1), shift(own, "z", -1), shift(own, "z", 4)
    pairs = [shift(jnp.stack([below, own]), "z", 2), shift(jnp.stack([own, above]), "z", -2)]
    prepared = own_cols(near)
    chunks = []
    chunks.append(own_chunk([own, below, above, far], prepared, (0,)))
    same = jnp.concatenate([jnp.stack([own, below, above, far]), *pairs])
    other = shift(same, "c", 1)
    chunks.append(own_chunk(pairs, prepared, (1,)))
    chunks.append(own_chunk([other], prepared, THEIRS))
    pieces, highs, lows, left, left_sq = [list(part) for part in zip(*chunks)]
    lefts = [*left, *left_sq]
    for cols in (behind, ahead):
        piece, high, low = more_chunk(ALL, cols, lefts, pieces)
        pieces = [piece]
        highs.append(high)
        lows.append(low)
    theirs, high_theirs, low_theirs = more_chunk(THEIRS, across, lefts, pieces, True)
    theirs = shift(theirs, "c", 1)
    mine, high_mine, low_mine = more_chunk(MINE, across, lefts, pieces, True)
    highs += [high_mine, high_theirs]
    lows += [low_mine, low_theirs]
    arrived = exchange(mine + theirs, "z")
    first, wide = between(aux, arrived, targets)
    gathered = exchange(wide, ("x", "y"))
    theirs = shift(second(THEIRS, gathered, highs, lows), "c", 1)
    mine = second(MINE, gathered, highs, lows)
    arrived = exchange(mine + theirs, "z")
    second_image, dots = settle(aux, arrived, targets, first)
    sums = jnp.sum(to_each(dots[0:1], ("y", "c")), axis=0)
    return tuple(finish(to_each(sums, ("x", "z")), targets, first, second_image))


def solution(mesh):
    finer = Mesh(mesh.devices.reshape(4, 8, 2, mesh.shape["row"]), AXES)
    spec = P(None, AXES)

    return jax.shard_map(
        on_device, mesh=finer, in_specs=(spec, spec, P(), P(), P()), out_specs=(spec, spec), check_vma=False
    )
```
